512 devices in a mesh: row: 8 (over x, core), col: 16 (over z_hi, y), layer: 4 (over z_lo).
Axes of the slice: x: 4, y: 4, z: 16 (z_hi: 4, z_lo: 4; z = z_hi * 4 + z_lo), core: 2. Of those that a mesh axis runs over, the one named last changes fastest.
Arguments:
- a_tiles: bfloat16 [8, 64, 128, 4096], P('row', ('col', 'layer')), may hold values from -0.109375 to 0.109375
- a_rows: int32 [8, 64, 128], P('row', ('col', 'layer')), may hold values from 0 to 127
- a_cols: int32 [8, 64, 128], P('row', ('col', 'layer')), may hold values from 0 to 15
- a_count: int32 [8, 64], P('row', ('col', 'layer')), may hold values from 16 to 128, as said below
- p_tiles: bfloat16 [16, 64, 4, 4096], P('row', ('col', 'layer')), may hold values from -0.375 to 0.375
- p_cols: int32 [16, 64, 4], P('row', ('col', 'layer')), may hold values from -1 to 1
Outputs:
- coarse: float32 [64, 192], replicated
The draws below stay inside these ranges and needn't reach their ends.
Inputs may be any that keep to these rules, and one draw needn't show every extreme that they name: `a_count`: some device uses all 128 slots and some device only 16 of them.
All inputs are finite; a program needn't handle non-finite values.
Results may differ from the reference program's by a relative error of at most 0.0037.
Values may be sent and summed in bfloat16 or wider, within the bound.
No kernel may reach another device: no remote copies, remote signals or barrier semaphores. Data moves between devices by JAX's collectives and lax.ppermute only.
A program may use at most 64 MiB of HBM per device.

```python
import jax
import jax.numpy as jnp
from jax import lax

TILE = 64
NP = 4
PB = 1
KR = 2
SA = 128
NKG = 64
FR = 128
KC = 16
NF = 1024
W = 2
N_ROW = 8


def draw_a_count(key, part):
    first_key, second_key, third_key = jax.random.split(key, 3)
    device_total = N_ROW * NKG
    light_counts = jax.random.randint(first_key, (device_total,), SA // 8, SA // 2 + 1)
    heavy_mask = jax.random.randint(second_key, (device_total,), 0, 16) == 0
    counts = jnp.where(heavy_mask, SA, light_counts)
    chosen_spots = jax.random.permutation(third_key, device_total)
    counts = counts.at[chosen_spots[0]].set(SA)
    counts = counts.at[chosen_spots[1]].set(SA // 8)
    return counts.reshape(N_ROW, NKG).astype(jnp.int32)


def draw_a_rows(key, part):
    near_key, far_key, pick_key, layer_key = jax.random.split(jax.random.fold_in(key, 71), 4)
    shape = (N_ROW, NKG, SA)
    near_offset = jax.random.randint(near_key, shape, -1, 2)
    far_group = jax.random.randint(far_key, shape, 0, NKG)
    pick_near = jax.random.randint(pick_key, shape, 0, 2) == 0
    own_group = jnp.arange(NKG, dtype=jnp.int32)[None, :, None]
    residue = jnp.where(pick_near, (own_group + near_offset + NKG) % NKG, far_group)
    row_layer = jax.random.randint(layer_key, shape, 0, KR)
    return (row_layer * NKG + residue).astype(jnp.int32)


def touch_ends(values, own_key, low, largest):
    spot = [jax.random.randint(jax.random.fold_in(own_key, axis), (), 0, length) for axis, length in enumerate(values.shape)]
    main_axis = values.shape.index(max(values.shape))
    beside = spot[:main_axis] + [(spot[main_axis] + 1) % values.shape[main_axis]] + spot[main_axis + 1:]
    return values.at[tuple(spot)].set(low).at[tuple(beside)].set(largest)


def levels(rng, dims, cuts, least, largest):
    def one(position, parts):
        heights = jax.random.uniform(jax.random.fold_in(jax.random.fold_in(rng, 6), position), (parts,), jnp.float32, least / len(cuts), largest / len(cuts))
        return jnp.repeat(jnp.exp(heights), dims[position] // parts).reshape((-1,) + (1,) * (len(dims) - position - 1))

    gain = one(*cuts[0])
    for cut in cuts[1:]:
        gain = gain * one(*cut)
    return gain


def gaussian(stream_key, shape, spread, bound, pieces=(), held_as=jnp.bfloat16):
    level = levels(stream_key, shape, pieces, -0.22, 0.18) if pieces else 1.0
    values = jax.random.normal(stream_key, shape, jnp.float32) * spread * level
    return jnp.minimum(jnp.maximum(values, -bound), bound).astype(held_as)


def setup_inputs(seed: int = 0) -> dict:
    key_list = jax.random.split(jax.random.key(seed), 7)
    return {
        "a_tiles": gaussian(key_list[0], (N_ROW, NKG, SA, TILE * TILE), (SA // KR * NF // 20) ** -0.5, 0.109375, ((0, 8), (1, 64))),
        "a_rows": draw_a_rows(jax.random.fold_in(key_list[6], 71), 0),
        "a_cols": touch_ends(jax.random.randint(key_list[2], (N_ROW, NKG, SA), 0, KC), jax.random.fold_in(key_list[2], 1), 0, KC - 1).astype(jnp.int32),
        "a_count": draw_a_count(jax.random.fold_in(key_list[6], 71), 0),
        "p_tiles": gaussian(key_list[4], (KC, NKG, NP, TILE * TILE), (TILE * NP) ** -0.5, 0.375, ((0, 8), (1, 64))),
        "p_cols": touch_ends(jax.random.randint(key_list[5], (KC, NKG, NP), -1, W), jax.random.fold_in(key_list[5], 1), -1, W - 1).astype(jnp.int32),
    }


def reference(a_tiles, a_rows, a_cols, a_count, p_tiles, p_cols):
    window_width = W * TILE
    onehot = (p_cols[..., None] == jnp.arange(W, dtype=jnp.int32)).astype(jnp.float32)
    tile_values = p_tiles.astype(jnp.float32).reshape(KC, NKG, NP, TILE, TILE)
    window = jnp.einsum('tfsj,tfsab->tfajb', onehot, tile_values)
    window = window.reshape(KC, NKG, TILE, window_width).astype(jnp.bfloat16)
    slot_ids = jnp.arange(SA, dtype=jnp.int32)

    def visit_device(running, device_inputs):
        device_index, tiles_dev, rows_dev, cols_dev, live_count = device_inputs
        row_group = device_index // NKG
        col_group = device_index % NKG
        picked = window[cols_dev, col_group].astype(jnp.float32)
        live_mask = (slot_ids < live_count).astype(jnp.float32)
        masked = tiles_dev.astype(jnp.float32).reshape(SA, TILE, TILE) * live_mask[:, None, None]
        products = jnp.einsum('sab,sbc->sac', masked, picked)
        row_block = jnp.zeros((FR, TILE, window_width), jnp.float32).at[rows_dev].add(products)
        first_row = (row_group * FR).astype(jnp.int32)
        current = lax.dynamic_slice_in_dim(running, first_row, FR, 0)
        running = lax.dynamic_update_slice_in_dim(running, current + row_block, first_row, 0)
        return running, None

    device_inputs = (
        jnp.arange(N_ROW * NKG, dtype=jnp.int32),
        a_tiles.reshape(N_ROW * NKG, SA, TILE * TILE),
        a_rows.reshape(N_ROW * NKG, SA),
        a_cols.reshape(N_ROW * NKG, SA),
        a_count.reshape(N_ROW * NKG),
    )
    product, _ = lax.scan(visit_device, jnp.zeros((NF, TILE, window_width), jnp.float32), device_inputs)
    prolong = window.reshape(NF * TILE, window_width).astype(jnp.float32)
    galerkin = jnp.dot(prolong.T, product.reshape(NF * TILE, window_width), precision=lax.Precision.HIGHEST)
    panel_size = PB * TILE
    return jnp.concatenate([galerkin[:panel_size, :panel_size], galerkin[:panel_size, panel_size:], galerkin[panel_size:, panel_size:]], axis=1)
```

```python
import jax
import jax.numpy as jnp
from jax import lax
from jax.experimental import pallas as pl
from jax.experimental.pallas import tpu as pltpu
from jax.sharding import Mesh
from jax.sharding import PartitionSpec as P

TILE = 64
HALF = TILE // 2
LANES = 2 * TILE
CHUNK = 16
GROUP = 4
COL_LAYER = ("zh", "y", "zl")
Z = ("zh", "zl")
ROW_Y = ("row", "y")


def lane_swapped(x):
    return pltpu.roll(x, TILE, axis=1)


def window_kernel(cols, p_ref, rows_ref, turned_ref, sums, natural):
    local_rows, slots = cols.shape
    lane = lax.broadcasted_iota(jnp.int32, (HALF, LANES), 1)
    for t in range(local_rows):
        tiles = p_ref[t].astype(jnp.float32)
        slot = lax.broadcasted_iota(jnp.int32, tiles.shape, 0)
        for j in range(2):
            chosen = jnp.zeros(tiles.shape, jnp.bool_)
            for s in range(slots):
                chosen = chosen | ((slot == s) & (cols[t, s] == j))
            total = jnp.sum(jnp.where(chosen, tiles, 0.0), axis=0, keepdims=True)
            for k in range(HALF):
                sums[t, j, k : k + 1] = total[:, k * LANES : (k + 1) * LANES]
    stacked = []
    for t in range(local_rows):
        first, second = sums[t, 0], sums[t, 1]
        even = jnp.where(lane < TILE, first, lane_swapped(second))
        odd = jnp.where(lane < TILE, lane_swapped(first), second)
        natural[t, pl.ds(0, HALF, stride=2)] = even
        natural[t, pl.ds(1, HALF, stride=2)] = odd
        stacked += [even, odd]
    rows = natural[...].astype(jnp.bfloat16)
    turned = jnp.concatenate(stacked, axis=0).T.astype(jnp.bfloat16)
    for r in range(rows_ref.shape[0]):
        rows_ref[r] = rows
    for z in range(turned_ref.shape[0]):
        turned_ref[z] = turned


def product_kernel(rows, cols, count, a_ref, w_ref, out_ref, split, total):
    live = count[0]
    total[...] = jnp.zeros_like(total)

    def place(row):
        f = row & (TILE - 1)
        z = ((f >> 4) << 2) | (f & 3)
        return ((((f >> 2) & 3) * 16 + z) * 2) + (row >> 6)

    def chunk(turn, carry):
        first = pl.multiple_of(turn * CHUNK, CHUNK)
        tiles = a_ref[pl.ds(first, CHUNK), :].astype(jnp.float32)
        slot = first + lax.broadcasted_iota(jnp.int32, tiles.shape, 0)
        tiles = jnp.where(slot < live, tiles, 0.0)
        for k in range(HALF):
            split[k] = tiles[:, k * LANES : (k + 1) * LANES]
        for g in range(0, CHUNK, GROUP):
            parts = []
            for i in range(g, g + GROUP):
                x = split[:, i, :]
                tile = jnp.concatenate([x, lane_swapped(x)], axis=0).astype(jnp.bfloat16)
                parts.append(
                    jnp.dot(
                        tile[:, :TILE], w_ref[cols[first + i]], preferred_element_type=jnp.float32
                    )
                )
            for i in range(g, g + GROUP):
                total[place(rows[first + i])] += parts[i - g]
        return carry

    lax.fori_loop(0, (live + CHUNK - 1) // CHUNK, chunk, 0)

    def store(turn, carry):
        out_ref[turn] = total[turn].astype(jnp.bfloat16)
        return carry

    lax.fori_loop(0, total.shape[0], store, 0, unroll=8)


def contract_kernel(p_ref, turned_ref, out_ref):
    peers, pieces = p_ref.shape[0], turned_ref.shape[0]
    galerkin = jnp.zeros((LANES, LANES), jnp.float32)
    for z in range(pieces):
        block = p_ref[0, z].astype(jnp.float32)
        for peer in range(1, peers):
            block += p_ref[peer, z].astype(jnp.float32)
        high = block.astype(jnp.bfloat16)
        low = (block - high.astype(jnp.float32)).astype(jnp.bfloat16)
        w = turned_ref[z]
        galerkin += jnp.dot(w, high, preferred_element_type=jnp.float32)
        galerkin += jnp.dot(w, low, preferred_element_type=jnp.float32)
    out_ref[:TILE] = galerkin[:TILE]
    out_ref[TILE:, :TILE] = galerkin[TILE : TILE + HALF, TILE:]
    out_ref[TILE:, TILE:] = galerkin[TILE + HALF :, TILE:]


def exchanged(x, axes):
    return lax.all_to_all(x, axes, 0, 0, tiled=True)


def summed_over_all(x):
    peers, depth = lax.axis_size(ROW_Y), lax.axis_size(Z)
    pieces = exchanged(x.reshape(peers, -1, LANES), ROW_Y)
    piece = jnp.sum(pieces, axis=0)
    piece = jnp.sum(exchanged(jnp.broadcast_to(piece, (depth, *piece.shape)), Z), axis=0)
    return exchanged(jnp.broadcast_to(piece, (peers, *piece.shape)), ROW_Y).reshape(x.shape)


def per_device(a_tiles, a_rows, a_cols, a_count, p_tiles, p_cols):
    local_rows, _, slots, area = p_tiles.shape
    total_slots = a_tiles.shape[2]
    n_row, n_y, n_z = lax.axis_size("row"), lax.axis_size("y"), lax.axis_size(Z)
    vmem = pl.BlockSpec(memory_space=pltpu.VMEM)
    own_rows, own_turned = pl.pallas_call(
        window_kernel,
        out_shape=(
            jax.ShapeDtypeStruct((n_row, local_rows, TILE, LANES), jnp.bfloat16),
            jax.ShapeDtypeStruct((n_z, LANES, LANES), jnp.bfloat16),
        ),
        grid_spec=pltpu.PrefetchScalarGridSpec(
            num_scalar_prefetch=1,
            in_specs=[vmem],
            out_specs=[vmem, vmem],
            scratch_shapes=[
                pltpu.VMEM((local_rows, 2, HALF, LANES), jnp.float32),
                pltpu.VMEM((local_rows, TILE, LANES), jnp.float32),
            ],
        ),
        name="window",
    )(p_cols.reshape(local_rows, slots), p_tiles.reshape(local_rows, slots, area))
    column_window = exchanged(own_rows, "row").reshape(n_row * local_rows, TILE, LANES)
    turned = exchanged(own_turned, Z)
    places = n_y * n_z * local_rows
    product = pl.pallas_call(
        product_kernel,
        out_shape=jax.ShapeDtypeStruct((places, TILE, LANES), jnp.bfloat16),
        grid_spec=pltpu.PrefetchScalarGridSpec(
            num_scalar_prefetch=3,
            in_specs=[vmem, vmem],
            out_specs=vmem,
            scratch_shapes=[
                pltpu.VMEM((HALF, CHUNK, LANES), jnp.float32),
                pltpu.VMEM((places, TILE, LANES), jnp.float32),
            ],
        ),
        name="product",
    )(
        a_rows.reshape(total_slots),
        a_cols.reshape(total_slots),
        a_count.reshape(1),
        a_tiles.reshape(total_slots, area),
        column_window,
    )
    gathered = exchanged(product.reshape(n_y, n_z, LANES, LANES), "y")
    galerkin = pl.pallas_call(
        contract_kernel,
        out_shape=jax.ShapeDtypeStruct((TILE + HALF, LANES), jnp.float32),
        in_specs=[vmem, vmem],
        out_specs=vmem,
        name="contract",
    )(gathered, turned)
    total = summed_over_all(galerkin)
    corner = jnp.concatenate([total[TILE:, :TILE], total[TILE:, TILE:]], axis=0)
    return jnp.concatenate([total[:TILE], corner], axis=1)


def solution(mesh):
    torus = Mesh(
        mesh.devices.reshape(mesh.shape["row"], 4, 4, mesh.shape["layer"]),
        ("row", "zh", "y", "zl"),
    )
    in_specs = (
        P("row", COL_LAYER, None, None),
        P("row", COL_LAYER, None),
        P("row", COL_LAYER, None),
        P("row", COL_LAYER),
        P("row", COL_LAYER, None, None),
        P("row", COL_LAYER, None),
    )
    return jax.shard_map(
        per_device, mesh=torus, in_specs=in_specs, out_specs=P(), check_vma=False
    )
```

```python
import jax
import jax.numpy as jnp
from jax import lax
from jax.experimental import pallas as pl
from jax.experimental.pallas import tpu as pltpu
from jax.sharding import Mesh
from jax.sharding import PartitionSpec as P

TILE = 64
HALF = TILE // 2
LANES = 2 * TILE
CHUNK = 16
GROUP = 4
COL_LAYER = ("zh", "y", "zl")
Z = ("zh", "zl")
ROW_Y = ("row", "y")
Y_ORDER = (1, 3, 2)


def lane_swapped(x):
    return pltpu.roll(x, TILE, axis=1)


def window_kernel(cols, p_ref, rows_ref, turned_ref, sums, natural):
    local_rows, slots = cols.shape
    lane = lax.broadcasted_iota(jnp.int32, (HALF, LANES), 1)
    for t in range(local_rows):
        tiles = p_ref[t].astype(jnp.float32)
        slot = lax.broadcasted_iota(jnp.int32, tiles.shape, 0)
        for j in range(2):
            chosen = jnp.zeros(tiles.shape, jnp.bool_)
            for s in range(slots):
                chosen = chosen | ((slot == s) & (cols[t, s] == j))
            total = jnp.sum(jnp.where(chosen, tiles, 0.0), axis=0, keepdims=True)
            for k in range(HALF):
                sums[t, j, k : k + 1] = total[:, k * LANES : (k + 1) * LANES]
    stacked = []
    for t in range(local_rows):
        first, second = sums[t, 0], sums[t, 1]
        even = jnp.where(lane < TILE, first, lane_swapped(second))
        odd = jnp.where(lane < TILE, lane_swapped(first), second)
        natural[t, pl.ds(0, HALF, stride=2)] = even
        natural[t, pl.ds(1, HALF, stride=2)] = odd
        stacked += [even, odd]
    rows = natural[...].astype(jnp.bfloat16)
    turned = jnp.concatenate(stacked, axis=0).T.astype(jnp.bfloat16)
    for r in range(rows_ref.shape[0]):
        rows_ref[r] = rows
    for z in range(turned_ref.shape[0]):
        turned_ref[z] = turned


def product_kernel(rows, cols, count, own_y, a_ref, w_ref, *refs):
    *out_refs, split, total = refs
    live = count[0]
    total[...] = jnp.zeros_like(total)

    def place(row):
        f = row & (TILE - 1)
        z = ((f >> 4) << 2) | (f & 3)
        distance = ((f >> 2) - own_y[0]) & 3
        return (distance * 16 + z) * 2 + (row >> 6)

    def chunk(turn, carry):
        first = pl.multiple_of(turn * CHUNK, CHUNK)
        tiles = a_ref[pl.ds(first, CHUNK), :].astype(jnp.float32)
        slot = first + lax.broadcasted_iota(jnp.int32, tiles.shape, 0)
        tiles = jnp.where(slot < live, tiles, 0.0)
        for k in range(HALF):
            split[k] = tiles[:, k * LANES : (k + 1) * LANES]
        for g in range(0, CHUNK, GROUP):
            parts = []
            for i in range(g, g + GROUP):
                x = split[:, i, :]
                tile = jnp.concatenate([x, lane_swapped(x)], axis=0).astype(jnp.bfloat16)
                parts.append(
                    jnp.dot(
                        tile[:, :TILE], w_ref[cols[first + i]], preferred_element_type=jnp.float32
                    )
                )
            for i in range(g, g + GROUP):
                total[place(rows[first + i])] += parts[i - g]
        return carry

    lax.fori_loop(0, (live + CHUNK - 1) // CHUNK, chunk, 0)

    for distance, out_ref in enumerate(out_refs):

        def store(turn, carry, out_ref=out_ref, first=distance * out_ref.shape[0]):
            out_ref[turn] = total[first + turn].astype(out_ref.dtype)
            return carry

        lax.fori_loop(0, out_ref.shape[0], store, 0, unroll=8)


def contract_kernel(*refs):
    *p_refs, turned_ref, out_ref = refs
    pieces = turned_ref.shape[0]
    galerkin = jnp.zeros((LANES, LANES), jnp.float32)
    for z in range(pieces):
        block = sum(p_ref[z].astype(jnp.float32) for p_ref in p_refs)
        high = block.astype(jnp.bfloat16)
        low = (block - high.astype(jnp.float32)).astype(jnp.bfloat16)
        w = turned_ref[z]
        galerkin += jnp.dot(w, high, preferred_element_type=jnp.float32)
        galerkin += jnp.dot(w, low, preferred_element_type=jnp.float32)
    out_ref[:TILE] = galerkin[:TILE]
    out_ref[TILE:, :TILE] = galerkin[TILE : TILE + HALF, TILE:]
    out_ref[TILE:, TILE:] = galerkin[TILE + HALF :, TILE:]


def exchanged(x, axes):
    return lax.all_to_all(x, axes, 0, 0, tiled=True)


def summed_over_all(x):
    peers, depth = lax.axis_size(ROW_Y), lax.axis_size(Z)
    pieces = exchanged(x.reshape(peers, -1, LANES), ROW_Y)
    piece = jnp.sum(pieces, axis=0)
    piece = jnp.sum(exchanged(jnp.broadcast_to(piece, (depth, *piece.shape)), Z), axis=0)
    return exchanged(jnp.broadcast_to(piece, (peers, *piece.shape)), ROW_Y).reshape(x.shape)


def coarse_blocks(a_tiles, a_rows, a_cols, a_count, p_tiles, p_cols):
    local_rows, _, slots, area = p_tiles.shape
    total_slots = a_tiles.shape[2]
    n_row, n_y, n_z = lax.axis_size("row"), lax.axis_size("y"), lax.axis_size(Z)
    vmem = pl.BlockSpec(memory_space=pltpu.VMEM)
    own_rows, own_turned = pl.pallas_call(
        window_kernel,
        out_shape=(
            jax.ShapeDtypeStruct((n_row, local_rows, TILE, LANES), jnp.bfloat16),
            jax.ShapeDtypeStruct((n_z, LANES, LANES), jnp.bfloat16),
        ),
        grid_spec=pltpu.PrefetchScalarGridSpec(
            num_scalar_prefetch=1,
            in_specs=[vmem],
            out_specs=[vmem, vmem],
            scratch_shapes=[
                pltpu.VMEM((local_rows, 2, HALF, LANES), jnp.float32),
                pltpu.VMEM((local_rows, TILE, LANES), jnp.float32),
            ],
        ),
        name="window",
    )(p_cols.reshape(local_rows, slots), p_tiles.reshape(local_rows, slots, area))
    column_window = exchanged(own_rows, "row").reshape(n_row * local_rows, TILE, LANES)
    turned = exchanged(own_turned, Z)
    places = n_z * local_rows
    products = pl.pallas_call(
        product_kernel,
        out_shape=[
            jax.ShapeDtypeStruct((places, TILE, LANES), jnp.bfloat16 if distance else jnp.float32)
            for distance in range(n_y)
        ],
        grid_spec=pltpu.PrefetchScalarGridSpec(
            num_scalar_prefetch=4,
            in_specs=[vmem, vmem],
            out_specs=[vmem] * n_y,
            scratch_shapes=[
                pltpu.VMEM((HALF, CHUNK, LANES), jnp.float32),
                pltpu.VMEM((n_y * places, TILE, LANES), jnp.float32),
            ],
        ),
        name="product",
    )(
        a_rows.reshape(total_slots),
        a_cols.reshape(total_slots),
        a_count.reshape(1),
        lax.axis_index("y").reshape(1),
        a_tiles.reshape(total_slots, area),
        column_window,
    )
    gathered = [products[0].reshape(n_z, LANES, LANES)]
    for distance in Y_ORDER:
        gathered.append(
            lax.ppermute(
                products[distance].reshape(n_z, LANES, LANES),
                "y",
                [(y, (y + distance) % n_y) for y in range(n_y)],
            )
        )
    galerkin = pl.pallas_call(
        contract_kernel,
        out_shape=jax.ShapeDtypeStruct((TILE + HALF, LANES), jnp.float32),
        in_specs=[vmem] * (n_y + 1),
        out_specs=vmem,
        name="contract",
    )(*gathered, turned)
    total = summed_over_all(galerkin)
    corner = jnp.concatenate([total[TILE:, :TILE], total[TILE:, TILE:]], axis=0)
    return jnp.concatenate([total[:TILE], corner], axis=1)


def solution(mesh):
    torus = Mesh(
        mesh.devices.reshape(mesh.shape["row"], 4, 4, mesh.shape["layer"]),
        ("row", "zh", "y", "zl"),
    )
    in_specs = (
        P("row", COL_LAYER, None, None),
        P("row", COL_LAYER, None),
        P("row", COL_LAYER, None),
        P("row", COL_LAYER),
        P("row", COL_LAYER, None, None),
        P("row", COL_LAYER, None),
    )
    return jax.shard_map(
        coarse_blocks, mesh=torus, in_specs=in_specs, out_specs=P(), check_vma=False
    )
```

```python
import jax
import jax.numpy as jnp
from jax import lax
from jax.experimental import pallas as pl
from jax.experimental.pallas import tpu as pltpu
from jax.sharding import Mesh
from jax.sharding import PartitionSpec as P

TILE = 64
HALF = TILE // 2
LANES = 2 * TILE
CHUNK = 16
GROUP = 4
COL_LAYER = ("zh", "y", "zl")
Z = ("zh", "zl")
ROW_Y = ("row", "y")
FAR = (0, 8, 4, 12)
NEAR = (0, 1, 15, 2)
VMEM = pl.BlockSpec(memory_space=pltpu.VMEM)
ANY = pl.BlockSpec(memory_space=pl.ANY)


def lane_swapped(x):
    return pltpu.roll(x, TILE, axis=1)


def window_kernel(cols, p_ref, rows_ref, turned_ref, split, natural):
    local_rows, slots = cols.shape
    lane = lax.broadcasted_iota(jnp.int32, (HALF, LANES), 1)
    panel = lax.broadcasted_iota(jnp.int32, (8, slots), 0)
    slot = lax.broadcasted_iota(jnp.int32, (8, slots), 1)
    stacked = []
    for t in range(local_rows):
        chosen = jnp.zeros((8, slots), jnp.float32)
        for s in range(slots):
            chosen = jnp.where((slot == s) & (panel == cols[t, s]), 1.0, chosen)
        sums = jnp.dot(chosen.astype(jnp.bfloat16), p_ref[t], preferred_element_type=jnp.float32)
        for k in range(HALF):
            split[t, k] = sums[:, k * LANES : (k + 1) * LANES]
        first, second = split[t, :, 0, :], split[t, :, 1, :]
        even = jnp.where(lane < TILE, first, lane_swapped(second))
        odd = jnp.where(lane < TILE, lane_swapped(first), second)
        natural[t, pl.ds(0, HALF, stride=2)] = even
        natural[t, pl.ds(1, HALF, stride=2)] = odd
        stacked += [even, odd]
    rows = natural[...].astype(jnp.bfloat16)
    for r in range(rows_ref.shape[0]):
        rows_ref[r] = rows
    turned_ref[0] = jnp.concatenate(stacked, axis=0).T.astype(jnp.bfloat16)


def unfold_kernel(count, a_ref, out_ref, split):
    first = pl.program_id(0) * CHUNK
    tiles = a_ref[...].astype(jnp.float32)
    slot = first + lax.broadcasted_iota(jnp.int32, tiles.shape, 0)
    tiles = jnp.where(slot < count[0], tiles, 0.0)
    for k in range(HALF):
        split[k] = tiles[:, k * LANES : (k + 1) * LANES]
    for i in range(CHUNK):
        x = split[:, i, :]
        out_ref[i] = jnp.concatenate([x, lane_swapped(x)], axis=0).astype(jnp.bfloat16)


def product_kernel(rows, cols, count, a_ref, w_hbm, out_hbm, window, total, rounded, w_sem, sems):
    step = pl.program_id(0)
    first = step * CHUNK
    w_copy = pltpu.make_async_copy(w_hbm, window, w_sem)

    @pl.when(step == 0)
    def _():
        w_copy.start()
        total[...] = jnp.zeros_like(total)
        w_copy.wait()

    def place(row):
        f = row & (TILE - 1)
        block = (((f >> 2) & 3) * 4 + (f & 3)) * 4 + (f >> 4)
        return block * 2 + (row >> 6)

    @pl.when(first < count[0])
    def _():
        for g in range(0, CHUNK, GROUP):
            parts = [
                jnp.dot(
                    a_ref[i, :, :TILE],
                    window[cols[first + i]],
                    preferred_element_type=jnp.float32,
                )
                for i in range(g, g + GROUP)
            ]
            for i in range(g, g + GROUP):
                total[place(rows[first + i])] += parts[i - g]

    @pl.when(step == pl.num_programs(0) - 1)
    def _():
        copies = []
        peers, size = out_hbm.shape[0], out_hbm.shape[1]
        for y in range(peers):

            def store(turn, carry, y=y):
                rounded[y, turn] = total[y * size + turn].astype(jnp.bfloat16)
                return carry

            lax.fori_loop(0, size, store, 0, unroll=8)
            copies.append(pltpu.make_async_copy(rounded.at[y], out_hbm.at[y], sems.at[y]))
            copies[-1].start()
        for copy in copies:
            copy.wait()


def contract_kernel(own_z, p_hbm, *refs):
    *w_hbm, out_ref, p_buf, w_buf, p_sems, w_sems = refs
    copies = []
    for near, w in enumerate(w_hbm):
        zl = (own_z[0] - NEAR[near]) & 3
        source = p_hbm.at[:, pl.ds(zl * 4, 4)]
        copies.append(
            (
                pltpu.make_async_copy(source, p_buf.at[near], p_sems.at[near]),
                pltpu.make_async_copy(w, w_buf.at[near], w_sems.at[near]),
            )
        )
        for copy in copies[-1]:
            copy.start()
    galerkin = jnp.zeros((LANES, LANES), jnp.float32)
    for near in range(len(w_hbm)):
        for copy in copies[near]:
            copy.wait()
        for far in range(len(FAR)):
            zh = ((own_z[0] - NEAR[near] - FAR[far]) >> 2) & 3
            block = sum(
                p_buf[near, y, zh].astype(jnp.float32) for y in range(p_buf.shape[1])
            )
            high = block.astype(jnp.bfloat16)
            low = (block - high.astype(jnp.float32)).astype(jnp.bfloat16)
            w = w_buf[near, far]
            galerkin += jnp.dot(w, high, preferred_element_type=jnp.float32)
            galerkin += jnp.dot(w, low, preferred_element_type=jnp.float32)
    out_ref[:, 0, :] = galerkin[:HALF]
    out_ref[:, 1, :] = galerkin[HALF:TILE]
    corner = galerkin[TILE:]
    lane = lax.broadcasted_iota(jnp.int32, (HALF, LANES), 1)
    out_ref[:, 2, :] = jnp.where(lane < TILE, lane_swapped(corner[:HALF]), corner[HALF:])


def exchanged(x, axes):
    return lax.all_to_all(x, axes, 0, 0, tiled=True)


def moved_along_z(x, distance):
    depth = lax.axis_size(Z)
    return lax.ppermute(x, Z, [(z, (z + distance) % depth) for z in range(depth)])


def summed_over_all(x):
    peers, depth = lax.axis_size(ROW_Y), lax.axis_size(Z)
    piece = jnp.sum(exchanged(x, ROW_Y), axis=0)
    piece = jnp.sum(exchanged(jnp.broadcast_to(piece, (depth, *piece.shape)), Z), axis=0)
    return exchanged(jnp.broadcast_to(piece, (peers, *piece.shape)), ROW_Y)


def coarse_blocks(a_tiles, a_rows, a_cols, a_count, p_tiles, p_cols):
    local_rows, _, slots, area = p_tiles.shape
    total_slots = a_tiles.shape[2]
    n_row, n_y = lax.axis_size("row"), lax.axis_size("y")
    count = a_count.reshape(1)
    own_rows, own_turned = pl.pallas_call(
        window_kernel,
        out_shape=(
            jax.ShapeDtypeStruct((n_row, local_rows, TILE, LANES), jnp.bfloat16),
            jax.ShapeDtypeStruct((1, LANES, LANES), jnp.bfloat16),
        ),
        grid_spec=pltpu.PrefetchScalarGridSpec(
            num_scalar_prefetch=1,
            in_specs=[VMEM],
            out_specs=[VMEM, VMEM],
            scratch_shapes=[
                pltpu.VMEM((local_rows, HALF, 8, LANES), jnp.float32),
                pltpu.VMEM((local_rows, TILE, LANES), jnp.float32),
            ],
        ),
        name="window",
    )(p_cols.reshape(local_rows, slots), p_tiles.reshape(local_rows, slots, area))
    column_window = exchanged(own_rows, "row").reshape(n_row * local_rows, TILE, LANES)
    unfolded = pl.pallas_call(
        unfold_kernel,
        out_shape=jax.ShapeDtypeStruct((total_slots, TILE, LANES), jnp.bfloat16),
        grid_spec=pltpu.PrefetchScalarGridSpec(
            num_scalar_prefetch=1,
            grid=(total_slots // CHUNK,),
            in_specs=[pl.BlockSpec((CHUNK, area), lambda i, *_: (i, 0))],
            out_specs=pl.BlockSpec((CHUNK, TILE, LANES), lambda i, *_: (i, 0, 0)),
            scratch_shapes=[pltpu.VMEM((HALF, CHUNK, LANES), jnp.float32)],
        ),
        name="unfold",
    )(count, a_tiles.reshape(total_slots, area))
    depth = lax.axis_size(Z)
    places = depth * local_rows
    product = pl.pallas_call(
        product_kernel,
        out_shape=jax.ShapeDtypeStruct((n_y, places, TILE, LANES), jnp.bfloat16),
        grid_spec=pltpu.PrefetchScalarGridSpec(
            num_scalar_prefetch=3,
            grid=(total_slots // CHUNK,),
            in_specs=[pl.BlockSpec((CHUNK, TILE, LANES), lambda i, *_: (i, 0, 0)), ANY],
            out_specs=ANY,
            scratch_shapes=[
                pltpu.VMEM((n_row * local_rows, TILE, LANES), jnp.bfloat16),
                pltpu.VMEM((n_y * places, TILE, LANES), jnp.float32),
                pltpu.VMEM((n_y, places, TILE, LANES), jnp.bfloat16),
                pltpu.SemaphoreType.DMA,
                pltpu.SemaphoreType.DMA((n_y,)),
            ],
        ),
        name="product",
    )(
        a_rows.reshape(total_slots),
        a_cols.reshape(total_slots),
        count,
        unfolded,
        column_window,
    )
    gathered = exchanged(product.reshape(n_y, depth, LANES, LANES), "y")
    far = [own_turned]
    for distance in FAR[1:]:
        far.append(moved_along_z(own_turned, distance))
    pieces = [jnp.concatenate(far, axis=0)]
    for distance in NEAR[1:]:
        pieces.append(moved_along_z(pieces[0], distance))
    galerkin = pl.pallas_call(
        contract_kernel,
        out_shape=jax.ShapeDtypeStruct((HALF, 3, LANES), jnp.float32),
        grid_spec=pltpu.PrefetchScalarGridSpec(
            num_scalar_prefetch=1,
            in_specs=[ANY] * (1 + len(NEAR)),
            out_specs=VMEM,
            scratch_shapes=[
                pltpu.VMEM((len(NEAR), n_y, len(FAR), LANES, LANES), jnp.bfloat16),
                pltpu.VMEM((len(NEAR), len(FAR), LANES, LANES), jnp.bfloat16),
                pltpu.SemaphoreType.DMA((len(NEAR),)),
                pltpu.SemaphoreType.DMA((len(NEAR),)),
            ],
        ),
        name="contract",
    )(lax.axis_index(Z).reshape(1), gathered, *pieces)
    total = summed_over_all(galerkin)
    corner = jnp.concatenate([total[:, 2, :TILE], total[:, 2, TILE:]], axis=0)
    upper = jnp.concatenate([total[:, 0], total[:, 1]], axis=0)
    return jnp.concatenate([upper, corner], axis=1)


def solution(mesh):
    torus = Mesh(
        mesh.devices.reshape(mesh.shape["row"], 4, 4, mesh.shape["layer"]),
        ("row", "zh", "y", "zl"),
    )
    in_specs = (
        P("row", COL_LAYER, None, None),
        P("row", COL_LAYER, None),
        P("row", COL_LAYER, None),
        P("row", COL_LAYER),
        P("row", COL_LAYER, None, None),
        P("row", COL_LAYER, None),
    )
    return jax.shard_map(coarse_blocks, mesh=torus, in_specs=in_specs, out_specs=P(), check_vma=False)
```

```python
import jax
import jax.numpy as jnp
from jax import lax
from jax.experimental import pallas as pl
from jax.experimental.pallas import tpu as pltpu
from jax.sharding import Mesh
from jax.sharding import PartitionSpec as P

TILE = 64
HALF = TILE // 2
LANES = 2 * TILE
CHUNK = 16
GROUP = 4
COL_LAYER = ("zh", "y", "zl")
Z = ("zh", "zl")
ROW_Y = ("row", "y")
PARTS = 4
VMEM = pl.BlockSpec(memory_space=pltpu.VMEM)
ANY = pl.BlockSpec(memory_space=pl.ANY)
HBM = pl.BlockSpec(memory_space=pltpu.HBM)


def lane_swapped(x):
    return pltpu.roll(x, TILE, axis=1)


def window_kernel(cols, p_ref, rows_ref, turned_ref, split, natural):
    local_rows, slots = cols.shape
    lane = lax.broadcasted_iota(jnp.int32, (HALF, LANES), 1)
    panel = lax.broadcasted_iota(jnp.int32, (8, slots), 0)
    slot = lax.broadcasted_iota(jnp.int32, (8, slots), 1)
    stacked = []
    for t in range(local_rows):
        chosen = jnp.zeros((8, slots), jnp.float32)
        for s in range(slots):
            chosen = jnp.where((slot == s) & (panel == cols[t, s]), 1.0, chosen)
        sums = jnp.dot(chosen.astype(jnp.bfloat16), p_ref[t], preferred_element_type=jnp.float32)
        for k in range(HALF):
            split[t, k] = sums[:, k * LANES : (k + 1) * LANES]
        first, second = split[t, :, 0, :], split[t, :, 1, :]
        even = jnp.where(lane < TILE, first, lane_swapped(second))
        odd = jnp.where(lane < TILE, lane_swapped(first), second)
        natural[t, pl.ds(0, HALF, stride=2)] = even
        natural[t, pl.ds(1, HALF, stride=2)] = odd
        stacked += [even, odd]
    rows = natural[...].astype(jnp.bfloat16)
    for r in range(rows_ref.shape[0]):
        rows_ref[r] = rows
    turned = jnp.concatenate(stacked, axis=0).T.astype(jnp.bfloat16)
    for z in range(turned_ref.shape[0]):
        turned_ref[z] = turned


def product_kernel(rows, cols, count, own_y, a_hbm, w_hbm, *refs):
    *out_hbm, tiles_in, window, split, total, rounded, in_sems, out_sems = refs
    live = count[0]
    in_copies = [
        pltpu.make_async_copy(a_hbm, tiles_in, in_sems.at[0]),
        pltpu.make_async_copy(w_hbm, window, in_sems.at[1]),
    ]
    for copy in in_copies:
        copy.start()
    total[...] = jnp.zeros_like(total)
    for copy in in_copies:
        copy.wait()

    def place(row):
        f = row & (TILE - 1)
        z = ((f >> 4) << 2) | (f & 3)
        distance = ((f >> 2) - own_y[0]) & 3
        return (distance * 16 + z) * 2 + (row >> 6)

    def chunk(turn, carry):
        first = pl.multiple_of(turn * CHUNK, CHUNK)
        tiles = tiles_in[pl.ds(first, CHUNK), :].astype(jnp.float32)
        slot = first + lax.broadcasted_iota(jnp.int32, tiles.shape, 0)
        tiles = jnp.where(slot < live, tiles, 0.0)
        for k in range(HALF):
            split[k] = tiles[:, k * LANES : (k + 1) * LANES]
        for g in range(0, CHUNK, GROUP):
            parts = []
            for i in range(g, g + GROUP):
                x = split[:, i, :]
                tile = jnp.concatenate([x, lane_swapped(x)], axis=0).astype(jnp.bfloat16)
                parts.append(
                    jnp.dot(
                        tile[:, :TILE], window[cols[first + i]], preferred_element_type=jnp.float32
                    )
                )
            for i in range(g, g + GROUP):
                total[place(rows[first + i])] += parts[i - g]
        return carry

    lax.fori_loop(0, (live + CHUNK - 1) // CHUNK, chunk, 0)
    size = out_hbm[0].shape[0]
    out_copies = [pltpu.make_async_copy(total.at[pl.ds(0, size)], out_hbm[0], out_sems.at[0])]
    out_copies[0].start()
    for distance in range(1, len(out_hbm)):

        def store(turn, carry, distance=distance):
            rounded[distance - 1, turn] = total[distance * size + turn].astype(jnp.bfloat16)
            return carry

        lax.fori_loop(0, size, store, 0, unroll=8)
        copy = pltpu.make_async_copy(
            rounded.at[distance - 1], out_hbm[distance], out_sems.at[distance]
        )
        copy.start()
        out_copies.append(copy)
    for copy in out_copies:
        copy.wait()


def contract_kernel(own_hbm, *refs):
    *p_hbm, w_hbm, out_ref, own_buf, p_buf, w_buf, sems = refs
    pieces, parts = w_hbm.shape[0], sems.shape[0]
    size = pieces // parts
    copies = []
    for part in range(parts):
        there = pl.ds(part * size, size)
        pairs = [(own_hbm.at[there], own_buf.at[there]), (w_hbm.at[there], w_buf.at[there])]
        pairs += [(p.at[there], p_buf.at[i, there]) for i, p in enumerate(p_hbm)]
        copies.append(
            [pltpu.make_async_copy(*pair, sems.at[part, i]) for i, pair in enumerate(pairs)]
        )
        for copy in copies[-1]:
            copy.start()
    galerkin = jnp.zeros((LANES, LANES), jnp.float32)
    for part in range(parts):
        for copy in copies[part]:
            copy.wait()
        for z in range(part * size, (part + 1) * size):
            block = own_buf[z]
            for i in range(len(p_hbm)):
                block += p_buf[i, z].astype(jnp.float32)
            high = block.astype(jnp.bfloat16)
            low = (block - high.astype(jnp.float32)).astype(jnp.bfloat16)
            galerkin += jnp.dot(w_buf[z], high, preferred_element_type=jnp.float32)
            galerkin += jnp.dot(w_buf[z], low, preferred_element_type=jnp.float32)
    out_ref[:, 0, :] = galerkin[:HALF]
    out_ref[:, 1, :] = galerkin[HALF:TILE]
    corner = galerkin[TILE:]
    lane = lax.broadcasted_iota(jnp.int32, (HALF, LANES), 1)
    out_ref[:, 2, :] = jnp.where(lane < TILE, lane_swapped(corner[:HALF]), corner[HALF:])


def exchanged(x, axes):
    return lax.all_to_all(x, axes, 0, 0, tiled=True)


def summed_over_all(x):
    peers, depth = lax.axis_size(ROW_Y), lax.axis_size(Z)
    piece = jnp.sum(exchanged(x, ROW_Y), axis=0)
    piece = jnp.sum(exchanged(jnp.broadcast_to(piece, (depth, *piece.shape)), Z), axis=0)
    return exchanged(jnp.broadcast_to(piece, (peers, *piece.shape)), ROW_Y)


def coarse_blocks(a_tiles, a_rows, a_cols, a_count, p_tiles, p_cols):
    local_rows, _, slots, area = p_tiles.shape
    total_slots = a_tiles.shape[2]
    n_row, n_y = lax.axis_size("row"), lax.axis_size("y")
    depth = lax.axis_size(Z)
    places = depth * local_rows
    own_rows, own_turned = pl.pallas_call(
        window_kernel,
        out_shape=(
            jax.ShapeDtypeStruct((n_row, local_rows, TILE, LANES), jnp.bfloat16),
            jax.ShapeDtypeStruct((depth, LANES, LANES), jnp.bfloat16),
        ),
        grid_spec=pltpu.PrefetchScalarGridSpec(
            num_scalar_prefetch=1,
            in_specs=[VMEM],
            out_specs=[VMEM, VMEM],
            scratch_shapes=[
                pltpu.VMEM((local_rows, HALF, 8, LANES), jnp.float32),
                pltpu.VMEM((local_rows, TILE, LANES), jnp.float32),
            ],
        ),
        name="window",
    )(p_cols.reshape(local_rows, slots), p_tiles.reshape(local_rows, slots, area))
    column_window = exchanged(own_rows, "row").reshape(n_row * local_rows, TILE, LANES)
    turned = exchanged(own_turned, Z)
    products = pl.pallas_call(
        product_kernel,
        out_shape=[
            jax.ShapeDtypeStruct((places, TILE, LANES), jnp.bfloat16 if distance else jnp.float32)
            for distance in range(n_y)
        ],
        grid_spec=pltpu.PrefetchScalarGridSpec(
            num_scalar_prefetch=4,
            in_specs=[HBM, ANY],
            out_specs=[ANY] + [HBM] * (n_y - 1),
            scratch_shapes=[
                pltpu.VMEM((total_slots, area), jnp.bfloat16),
                pltpu.VMEM((n_row * local_rows, TILE, LANES), jnp.bfloat16),
                pltpu.VMEM((HALF, CHUNK, LANES), jnp.float32),
                pltpu.VMEM((n_y * places, TILE, LANES), jnp.float32),
                pltpu.VMEM((n_y - 1, places, TILE, LANES), jnp.bfloat16),
                pltpu.SemaphoreType.DMA((2,)),
                pltpu.SemaphoreType.DMA((n_y,)),
            ],
        ),
        compiler_params=pltpu.CompilerParams(vmem_limit_bytes=16 << 20),
        name="product",
    )(
        a_rows.reshape(total_slots),
        a_cols.reshape(total_slots),
        a_count.reshape(1),
        lax.axis_index("y").reshape(1),
        a_tiles.reshape(total_slots, area),
        column_window,
    )
    gathered = [products[0].reshape(depth, LANES, LANES)]
    for distance in range(1, n_y):
        gathered.append(
            lax.ppermute(
                products[distance].reshape(depth, LANES, LANES),
                "y",
                [(y, (y + distance) % n_y) for y in range(n_y)],
            )
        )
    galerkin = pl.pallas_call(
        contract_kernel,
        out_shape=jax.ShapeDtypeStruct((HALF, 3, LANES), jnp.float32),
        in_specs=[ANY] * (n_y + 1),
        out_specs=VMEM,
        scratch_shapes=[
            pltpu.VMEM((depth, LANES, LANES), jnp.float32),
            pltpu.VMEM((n_y - 1, depth, LANES, LANES), jnp.bfloat16),
            pltpu.VMEM((depth, LANES, LANES), jnp.bfloat16),
            pltpu.SemaphoreType.DMA((PARTS, n_y + 1)),
        ],
        compiler_params=pltpu.CompilerParams(vmem_limit_bytes=8 << 20),
        name="contract",
    )(*gathered, turned)
    total = summed_over_all(galerkin)
    corner = jnp.concatenate([total[:, 2, :TILE], total[:, 2, TILE:]], axis=0)
    upper = jnp.concatenate([total[:, 0], total[:, 1]], axis=0)
    return jnp.concatenate([upper, corner], axis=1)


def solution(mesh):
    torus = Mesh(
        mesh.devices.reshape(mesh.shape["row"], 4, 4, mesh.shape["layer"]),
        ("row", "zh", "y", "zl"),
    )
    in_specs = (
        P("row", COL_LAYER, None, None),
        P("row", COL_LAYER, None),
        P("row", COL_LAYER, None),
        P("row", COL_LAYER),
        P("row", COL_LAYER, None, None),
        P("row", COL_LAYER, None),
    )
    return jax.shard_map(
        coarse_blocks, mesh=torus, in_specs=in_specs, out_specs=P(), check_vma=False
    )
```

```python
import jax
import jax.numpy as jnp
from jax import lax
from jax.experimental import pallas as pl
from jax.experimental.pallas import tpu as pltpu
from jax.sharding import Mesh
from jax.sharding import PartitionSpec as P

TILE = 64
HALF = TILE // 2
LANES = 2 * TILE
CHUNK = 16
GROUP = 4
COL_LAYER = ("zh", "y", "zl")
Z = ("zh", "zl")
ROW_Y = ("row", "y")
VMEM = pl.BlockSpec(memory_space=pltpu.VMEM)
ANY = pl.BlockSpec(memory_space=pl.ANY)


def lane_swapped(x):
    return pltpu.roll(x, TILE, axis=1)


def window_kernel(cols, p_ref, rows_ref, turned_ref, split, natural):
    local_rows, slots = cols.shape
    lane = lax.broadcasted_iota(jnp.int32, (HALF, LANES), 1)
    panel = lax.broadcasted_iota(jnp.int32, (8, slots), 0)
    slot = lax.broadcasted_iota(jnp.int32, (8, slots), 1)
    stacked = []
    for t in range(local_rows):
        chosen = jnp.zeros((8, slots), jnp.float32)
        for s in range(slots):
            chosen = jnp.where((slot == s) & (panel == cols[t, s]), 1.0, chosen)
        sums = jnp.dot(chosen.astype(jnp.bfloat16), p_ref[t], preferred_element_type=jnp.float32)
        for k in range(HALF):
            split[t, k] = sums[:, k * LANES : (k + 1) * LANES]
        first, second = split[t, :, 0, :], split[t, :, 1, :]
        even = jnp.where(lane < TILE, first, lane_swapped(second))
        odd = jnp.where(lane < TILE, lane_swapped(first), second)
        natural[t, pl.ds(0, HALF, stride=2)] = even
        natural[t, pl.ds(1, HALF, stride=2)] = odd
        stacked += [even, odd]
    rows = natural[...].astype(jnp.bfloat16)
    for r in range(rows_ref.shape[0]):
        rows_ref[r] = rows
    turned = jnp.concatenate(stacked, axis=0).T.astype(jnp.bfloat16)
    for z in range(turned_ref.shape[0]):
        turned_ref[z] = turned


def product_kernel(rows, cols, count, own_y, a_hbm, window, *refs):
    *out_hbm, tiles_in, split, total, rounded, in_sem, out_sems = refs
    live = count[0]
    in_copy = pltpu.make_async_copy(a_hbm, tiles_in, in_sem)
    in_copy.start()
    total[...] = jnp.zeros_like(total)
    in_copy.wait()

    def place(row):
        f = row & (TILE - 1)
        z = ((f >> 4) << 2) | (f & 3)
        distance = ((f >> 2) - own_y[0]) & 3
        return (distance * 16 + z) * 2 + (row >> 6)

    def chunk(turn, carry):
        first = pl.multiple_of(turn * CHUNK, CHUNK)
        tiles = tiles_in[pl.ds(first, CHUNK), :].astype(jnp.float32)
        slot = first + lax.broadcasted_iota(jnp.int32, tiles.shape, 0)
        tiles = jnp.where(slot < live, tiles, 0.0)
        for k in range(HALF):
            split[k] = tiles[:, k * LANES : (k + 1) * LANES]
        for g in range(0, CHUNK, GROUP):
            parts = []
            for i in range(g, g + GROUP):
                x = split[:, i, :]
                tile = jnp.concatenate([x, lane_swapped(x)], axis=0).astype(jnp.bfloat16)
                parts.append(
                    jnp.dot(
                        tile[:, :TILE], window[cols[first + i]], preferred_element_type=jnp.float32
                    )
                )
            for i in range(g, g + GROUP):
                total[place(rows[first + i])] += parts[i - g]
        return carry

    lax.fori_loop(0, (live + CHUNK - 1) // CHUNK, chunk, 0)
    size = out_hbm[0].shape[0]
    out_copies = [pltpu.make_async_copy(total.at[pl.ds(0, size)], out_hbm[0], out_sems.at[0])]
    out_copies[0].start()
    for distance in range(1, len(out_hbm)):

        def store(turn, carry, distance=distance):
            rounded[distance - 1, turn] = total[distance * size + turn].astype(jnp.bfloat16)
            return carry

        lax.fori_loop(0, size, store, 0, unroll=8)
        copy = pltpu.make_async_copy(
            rounded.at[distance - 1], out_hbm[distance], out_sems.at[distance]
        )
        copy.start()
        out_copies.append(copy)
    for copy in out_copies:
        copy.wait()


def contract_kernel(own_ref, *refs):
    *p_refs, w_ref, out_ref = refs
    galerkin = jnp.zeros((LANES, LANES), jnp.float32)
    for z in range(w_ref.shape[0]):
        block = own_ref[z]
        for p_ref in p_refs:
            block += p_ref[z].astype(jnp.float32)
        high = block.astype(jnp.bfloat16)
        low = (block - high.astype(jnp.float32)).astype(jnp.bfloat16)
        galerkin += jnp.dot(w_ref[z], high, preferred_element_type=jnp.float32)
        galerkin += jnp.dot(w_ref[z], low, preferred_element_type=jnp.float32)
    out_ref[:, 0, :] = galerkin[:HALF]
    out_ref[:, 1, :] = galerkin[HALF:TILE]
    corner = galerkin[TILE:]
    lane = lax.broadcasted_iota(jnp.int32, (HALF, LANES), 1)
    out_ref[:, 2, :] = jnp.where(lane < TILE, lane_swapped(corner[:HALF]), corner[HALF:])


def in_vmem(x):
    return pltpu.with_memory_space_constraint(x, pltpu.VMEM)


def exchanged(x, axes):
    return lax.all_to_all(x, axes, 0, 0, tiled=True)


def summed_over_all(x):
    peers, depth = lax.axis_size(ROW_Y), lax.axis_size(Z)
    piece = jnp.sum(exchanged(x, ROW_Y), axis=0)
    piece = jnp.sum(exchanged(jnp.broadcast_to(piece, (depth, *piece.shape)), Z), axis=0)
    return exchanged(jnp.broadcast_to(piece, (peers, *piece.shape)), ROW_Y)


def coarse_blocks(a_tiles, a_rows, a_cols, a_count, p_tiles, p_cols):
    local_rows, _, slots, area = p_tiles.shape
    total_slots = a_tiles.shape[2]
    n_row, n_y = lax.axis_size("row"), lax.axis_size("y")
    depth = lax.axis_size(Z)
    places = depth * local_rows
    own_rows, own_turned = pl.pallas_call(
        window_kernel,
        out_shape=(
            jax.ShapeDtypeStruct((n_row, local_rows, TILE, LANES), jnp.bfloat16),
            jax.ShapeDtypeStruct((depth, LANES, LANES), jnp.bfloat16),
        ),
        grid_spec=pltpu.PrefetchScalarGridSpec(
            num_scalar_prefetch=1,
            in_specs=[VMEM],
            out_specs=[VMEM, VMEM],
            scratch_shapes=[
                pltpu.VMEM((local_rows, HALF, 8, LANES), jnp.float32),
                pltpu.VMEM((local_rows, TILE, LANES), jnp.float32),
            ],
        ),
        name="window",
    )(p_cols.reshape(local_rows, slots), p_tiles.reshape(local_rows, slots, area))
    column_window = exchanged(own_rows, "row").reshape(n_row * local_rows, TILE, LANES)
    turned = exchanged(own_turned, Z)
    products = pl.pallas_call(
        product_kernel,
        out_shape=[
            jax.ShapeDtypeStruct(
                (places, TILE, LANES), jnp.bfloat16 if distance else jnp.float32
            )
            for distance in range(n_y)
        ],
        grid_spec=pltpu.PrefetchScalarGridSpec(
            num_scalar_prefetch=4,
            in_specs=[ANY, VMEM],
            out_specs=[ANY] * n_y,
            scratch_shapes=[
                pltpu.VMEM((total_slots, area), jnp.bfloat16),
                pltpu.VMEM((HALF, CHUNK, LANES), jnp.float32),
                pltpu.VMEM((n_y * places, TILE, LANES), jnp.float32),
                pltpu.VMEM((n_y - 1, places, TILE, LANES), jnp.bfloat16),
                pltpu.SemaphoreType.DMA,
                pltpu.SemaphoreType.DMA((n_y,)),
            ],
        ),
        name="product",
    )(
        a_rows.reshape(total_slots),
        a_cols.reshape(total_slots),
        a_count.reshape(1),
        lax.axis_index("y").reshape(1),
        a_tiles.reshape(total_slots, area),
        in_vmem(column_window),
    )
    gathered = [products[0].reshape(depth, LANES, LANES)]
    for distance in range(1, n_y):
        gathered.append(
            lax.ppermute(
                products[distance].reshape(depth, LANES, LANES),
                "y",
                [(y, (y + distance) % n_y) for y in range(n_y)],
            )
        )
    galerkin = pl.pallas_call(
        contract_kernel,
        out_shape=jax.ShapeDtypeStruct((HALF, 3, LANES), jnp.float32),
        in_specs=[VMEM] * (n_y + 1),
        out_specs=VMEM,
        compiler_params=pltpu.CompilerParams(vmem_limit_bytes=8 << 20),
        name="contract",
    )(*[in_vmem(x) for x in (*gathered, turned)])
    total = summed_over_all(galerkin)
    corner = jnp.concatenate([total[:, 2, :TILE], total[:, 2, TILE:]], axis=0)
    upper = jnp.concatenate([total[:, 0], total[:, 1]], axis=0)
    return jnp.concatenate([upper, corner], axis=1)


def solution(mesh):
    torus = Mesh(
        mesh.devices.reshape(mesh.shape["row"], 4, 4, mesh.shape["layer"]),
        ("row", "zh", "y", "zl"),
    )
    in_specs = (
        P("row", COL_LAYER, None, None),
        P("row", COL_LAYER, None),
        P("row", COL_LAYER, None),
        P("row", COL_LAYER),
        P("row", COL_LAYER, None, None),
        P("row", COL_LAYER, None),
    )
    return jax.shard_map(coarse_blocks, mesh=torus, in_specs=in_specs, out_specs=P(), check_vma=False)
```

```python
import jax
import jax.numpy as jnp
from jax import lax
from jax.experimental import pallas as pl
from jax.experimental.pallas import tpu as pltpu
from jax.sharding import Mesh
from jax.sharding import PartitionSpec as P

TILE = 64
HALF = TILE // 2
LANES = 2 * TILE
CHUNK = 16
GROUP = 4
NEAR = (0, 1, 2, 15)
COL_LAYER = ("zh", "y", "zl")
Z = ("zh", "zl")
ROW_Y = ("row", "y")
VMEM = pl.BlockSpec(memory_space=pltpu.VMEM)
ANY = pl.BlockSpec(memory_space=pl.ANY)


def lane_swapped(x):
    return pltpu.roll(x, TILE, axis=1)


def window_kernel(cols, p_ref, rows_ref, turned_ref, split, natural):
    local_rows, slots = cols.shape
    lane = lax.broadcasted_iota(jnp.int32, (HALF, LANES), 1)
    panel = lax.broadcasted_iota(jnp.int32, (8, slots), 0)
    slot = lax.broadcasted_iota(jnp.int32, (8, slots), 1)
    stacked = []
    for t in range(local_rows):
        chosen = jnp.zeros((8, slots), jnp.float32)
        for s in range(slots):
            chosen = jnp.where((slot == s) & (panel == cols[t, s]), 1.0, chosen)
        sums = jnp.dot(chosen.astype(jnp.bfloat16), p_ref[t], preferred_element_type=jnp.float32)
        for k in range(HALF):
            split[t, k] = sums[:, k * LANES : (k + 1) * LANES]
        first, second = split[t, :, 0, :], split[t, :, 1, :]
        even = jnp.where(lane < TILE, first, lane_swapped(second))
        odd = jnp.where(lane < TILE, lane_swapped(first), second)
        natural[t, pl.ds(0, HALF, stride=2)] = even
        natural[t, pl.ds(1, HALF, stride=2)] = odd
        stacked += [even, odd]
    rows = natural[...].astype(jnp.bfloat16)
    for r in range(rows_ref.shape[0]):
        rows_ref[r] = rows
    turned = jnp.concatenate(stacked, axis=0).T.astype(jnp.bfloat16)
    for z in range(turned_ref.shape[0]):
        turned_ref[z] = turned


def unfold_kernel(tiles, out_ref, split):
    def chunk(turn, carry):
        first = pl.multiple_of(turn * CHUNK, CHUNK)
        some = tiles[pl.ds(first, CHUNK), :].astype(jnp.float32)
        for k in range(HALF):
            split[k] = some[:, k * LANES : (k + 1) * LANES]
        for i in range(CHUNK):
            x = split[:, i, :]
            out_ref[first + i] = jnp.concatenate([x, lane_swapped(x)], axis=0).astype(jnp.bfloat16)
        return carry

    lax.fori_loop(0, tiles.shape[0] // CHUNK, chunk, 0)


def product_kernel(slots, tiles, window, *refs):
    *out_hbm, total, rounded, out_sems = refs
    total[...] = jnp.zeros_like(total)

    def chunk(turn, carry):
        first = turn * CHUNK
        for g in range(0, CHUNK, GROUP):
            held = [slots[first + i] for i in range(g, g + GROUP)]
            parts = [
                jnp.dot(
                    tiles[first + g + i, :, :TILE],
                    window[held[i] & 15],
                    preferred_element_type=jnp.float32,
                )
                for i in range(GROUP)
            ]
            for i in range(GROUP):
                total[held[i] >> 4] += parts[i]
        return carry

    lax.fori_loop(0, tiles.shape[0] // CHUNK, chunk, 0)
    size = out_hbm[0].shape[0]
    out_copies = [pltpu.make_async_copy(total.at[pl.ds(0, size)], out_hbm[0], out_sems.at[0])]
    out_copies[0].start()
    for distance in range(1, len(out_hbm)):

        def store(turn, carry, distance=distance):
            rounded[distance - 1, turn] = total[distance * size + turn].astype(jnp.bfloat16)
            return carry

        lax.fori_loop(0, size, store, 0, unroll=8)
        copy = pltpu.make_async_copy(
            rounded.at[distance - 1], out_hbm[distance], out_sems.at[distance]
        )
        copy.start()
        out_copies.append(copy)
    for copy in out_copies:
        copy.wait()


def contract_kernel(*refs):
    p_refs, (*w_refs, out_ref) = refs[:4], refs[4:]
    galerkin = jnp.zeros((LANES, LANES), jnp.float32)
    for near, w_ref in enumerate(w_refs):
        for zh in range(w_ref.shape[0]):
            piece = near * w_ref.shape[0] + zh
            block = sum(p_ref[piece].astype(jnp.float32) for p_ref in p_refs)
            high = block.astype(jnp.bfloat16)
            low = (block - high.astype(jnp.float32)).astype(jnp.bfloat16)
            galerkin += jnp.dot(w_ref[zh], high, preferred_element_type=jnp.float32)
            galerkin += jnp.dot(w_ref[zh], low, preferred_element_type=jnp.float32)
    out_ref[:, 0, :] = galerkin[:HALF]
    out_ref[:, 1, :] = galerkin[HALF:TILE]
    corner = galerkin[TILE:]
    lane = lax.broadcasted_iota(jnp.int32, (HALF, LANES), 1)
    out_ref[:, 2, :] = jnp.where(lane < TILE, lane_swapped(corner[:HALF]), corner[HALF:])


def in_vmem(x):
    return pltpu.with_memory_space_constraint(x, pltpu.VMEM)


def exchanged(x, axes):
    return lax.all_to_all(x, axes, 0, 0, tiled=True)


def moved(x, axes, distance):
    peers = lax.axis_size(axes)
    return lax.ppermute(x, axes, [(i, (i + distance) % peers) for i in range(peers)])


def summed_over_all(x):
    peers, depth = lax.axis_size(ROW_Y), lax.axis_size(Z)
    piece = jnp.sum(exchanged(x, ROW_Y), axis=0)
    piece = jnp.sum(exchanged(jnp.broadcast_to(piece, (depth, *piece.shape)), Z), axis=0)
    return exchanged(jnp.broadcast_to(piece, (peers, *piece.shape)), ROW_Y)


def slot_table(a_rows, a_cols, a_count):
    rows, cols = a_rows.reshape(-1), a_cols.reshape(-1)
    f = rows % TILE
    zh, y, zl = f // 16, f // 4 % 4, f % 4
    y_distance = (y - lax.axis_index("y")) % 4
    z_distance = (lax.axis_index("zl") - zl) % 4
    place = ((y_distance * 4 + z_distance) * 4 + zh) * 2 + rows // TILE
    live = jnp.arange(rows.shape[0], dtype=jnp.int32) < a_count.reshape(())
    return jnp.where(live, place, 128) * 16 + cols


def coarse_blocks(a_tiles, a_rows, a_cols, a_count, p_tiles, p_cols):
    local_rows, _, slots, area = p_tiles.shape
    total_slots = a_tiles.shape[2]
    n_row, n_y = lax.axis_size("row"), lax.axis_size("y")
    n_zh, n_zl = lax.axis_size("zh"), lax.axis_size("zl")
    places = n_zh * n_zl * local_rows
    own_rows, own_turned = pl.pallas_call(
        window_kernel,
        out_shape=(
            jax.ShapeDtypeStruct((n_row, local_rows, TILE, LANES), jnp.bfloat16),
            jax.ShapeDtypeStruct((n_zh, LANES, LANES), jnp.bfloat16),
        ),
        grid_spec=pltpu.PrefetchScalarGridSpec(
            num_scalar_prefetch=1,
            in_specs=[VMEM],
            out_specs=[VMEM, VMEM],
            scratch_shapes=[
                pltpu.VMEM((local_rows, HALF, 8, LANES), jnp.float32),
                pltpu.VMEM((local_rows, TILE, LANES), jnp.float32),
            ],
        ),
        name="window",
    )(p_cols.reshape(local_rows, slots), p_tiles.reshape(local_rows, slots, area))
    column_window = exchanged(own_rows, "row").reshape(n_row * local_rows, TILE, LANES)
    unfolded = pl.pallas_call(
        unfold_kernel,
        out_shape=jax.ShapeDtypeStruct((total_slots, TILE, LANES), jnp.bfloat16),
        in_specs=[VMEM],
        out_specs=VMEM,
        scratch_shapes=[pltpu.VMEM((HALF, CHUNK, LANES), jnp.float32)],
        compiler_params=pltpu.CompilerParams(vmem_limit_bytes=8 << 20),
        name="unfold",
    )(in_vmem(a_tiles.reshape(total_slots, area)))
    pieces = [exchanged(own_turned, "zh")]
    products = pl.pallas_call(
        product_kernel,
        out_shape=[
            jax.ShapeDtypeStruct(
                (places, TILE, LANES), jnp.bfloat16 if distance else jnp.float32
            )
            for distance in range(n_y)
        ],
        grid_spec=pltpu.PrefetchScalarGridSpec(
            num_scalar_prefetch=1,
            in_specs=[VMEM, VMEM],
            out_specs=[ANY] * n_y,
            scratch_shapes=[
                pltpu.VMEM((n_y * places + 1, TILE, LANES), jnp.float32),
                pltpu.VMEM((n_y - 1, places, TILE, LANES), jnp.bfloat16),
                pltpu.SemaphoreType.DMA((n_y,)),
            ],
        ),
        name="product",
    )(slot_table(a_rows, a_cols, a_count), in_vmem(unfolded), in_vmem(column_window))
    gathered = [products[0].reshape(-1, LANES, LANES)]
    for distance in range(1, n_y):
        gathered.append(moved(products[distance].reshape(-1, LANES, LANES), "y", distance))
    for distance in NEAR[1:]:
        pieces.append(moved(pieces[0], Z, distance))
    galerkin = pl.pallas_call(
        contract_kernel,
        out_shape=jax.ShapeDtypeStruct((HALF, 3, LANES), jnp.float32),
        in_specs=[VMEM] * (n_y + n_zl),
        out_specs=VMEM,
        compiler_params=pltpu.CompilerParams(vmem_limit_bytes=8 << 20),
        name="contract",
    )(*[in_vmem(x) for x in (*gathered, *pieces)])
    total = summed_over_all(galerkin)
    corner = jnp.concatenate([total[:, 2, :TILE], total[:, 2, TILE:]], axis=0)
    upper = jnp.concatenate([total[:, 0], total[:, 1]], axis=0)
    return jnp.concatenate([upper, corner], axis=1)


def solution(mesh):
    torus = Mesh(
        mesh.devices.reshape(mesh.shape["row"], 4, 4, mesh.shape["layer"]),
        ("row", "zh", "y", "zl"),
    )
    in_specs = (
        P("row", COL_LAYER, None, None),
        P("row", COL_LAYER, None),
        P("row", COL_LAYER, None),
        P("row", COL_LAYER),
        P("row", COL_LAYER, None, None),
        P("row", COL_LAYER, None),
    )
    return jax.shard_map(coarse_blocks, mesh=torus, in_specs=in_specs, out_specs=P(), check_vma=False)
```

```python
import jax
import jax.numpy as jnp
from jax import lax
from jax.experimental import pallas as pl
from jax.experimental.pallas import tpu as pltpu
from jax.sharding import Mesh
from jax.sharding import PartitionSpec as P

TILE = 64
HALF = TILE // 2
LANES = 2 * TILE
CHUNK = 16
GROUP = 4
NEAR = (0, 1, 2, 15)
COL_LAYER = ("zh", "y", "zl")
Z = ("zh", "zl")
ROW_Y = ("row", "y")
VMEM = pl.BlockSpec(memory_space=pltpu.VMEM)
ANY = pl.BlockSpec(memory_space=pl.ANY)


def lane_swapped(x):
    return pltpu.roll(x, TILE, axis=1)


def window_kernel(cols, p_ref, rows_ref, turned_ref, split, natural):
    local_rows, slots = cols.shape
    lane = lax.broadcasted_iota(jnp.int32, (HALF, LANES), 1)
    panel = lax.broadcasted_iota(jnp.int32, (8, slots), 0)
    slot = lax.broadcasted_iota(jnp.int32, (8, slots), 1)
    stacked = []
    for t in range(local_rows):
        chosen = jnp.zeros((8, slots), jnp.float32)
        for s in range(slots):
            chosen = jnp.where((slot == s) & (panel == cols[t, s]), 1.0, chosen)
        sums = jnp.dot(chosen.astype(jnp.bfloat16), p_ref[t], preferred_element_type=jnp.float32)
        for k in range(HALF):
            split[t, k] = sums[:, k * LANES : (k + 1) * LANES]
        first, second = split[t, :, 0, :], split[t, :, 1, :]
        even = jnp.where(lane < TILE, first, lane_swapped(second))
        odd = jnp.where(lane < TILE, lane_swapped(first), second)
        natural[t, pl.ds(0, HALF, stride=2)] = even
        natural[t, pl.ds(1, HALF, stride=2)] = odd
        stacked += [even, odd]
    rows = natural[...].astype(jnp.bfloat16)
    for r in range(rows_ref.shape[0]):
        rows_ref[r] = rows
    turned = jnp.concatenate(stacked, axis=0).T.astype(jnp.bfloat16)
    for z in range(turned_ref.shape[0]):
        turned_ref[z] = turned


def unfold_kernel(tiles, out_ref, split):
    def chunk(turn, carry):
        first = pl.multiple_of(turn * CHUNK, CHUNK)
        some = tiles[pl.ds(first, CHUNK), :].astype(jnp.float32)
        for k in range(HALF):
            split[k] = some[:, k * LANES : (k + 1) * LANES]
        for i in range(CHUNK):
            x = split[:, i, :]
            out_ref[first + i] = jnp.concatenate([x, lane_swapped(x)], axis=0).astype(jnp.bfloat16)
        return carry

    lax.fori_loop(0, tiles.shape[0] // CHUNK, chunk, 0)


def product_kernel(slots, tiles, window, *refs):
    *out_hbm, total, rounded, out_sems = refs
    total[...] = jnp.zeros_like(total)

    def chunk(turn, carry):
        first = turn * CHUNK
        for g in range(0, CHUNK, GROUP):
            held = [slots[first + i] for i in range(g, g + GROUP)]
            parts = [
                jnp.dot(
                    tiles[first + g + i, :, :TILE],
                    window[held[i] & 15],
                    preferred_element_type=jnp.float32,
                )
                for i in range(GROUP)
            ]
            for i in range(GROUP):
                total[held[i] >> 4] += parts[i]
        return carry

    lax.fori_loop(0, tiles.shape[0] // CHUNK, chunk, 0)
    size = out_hbm[0].shape[0]
    out_copies = [pltpu.make_async_copy(total.at[pl.ds(0, size)], out_hbm[0], out_sems.at[0])]
    out_copies[0].start()
    for distance in range(1, len(out_hbm)):

        def store(turn, carry, distance=distance):
            rounded[distance - 1, turn] = total[distance * size + turn].astype(jnp.bfloat16)
            return carry

        lax.fori_loop(0, size, store, 0, unroll=8)
        copy = pltpu.make_async_copy(
            rounded.at[distance - 1], out_hbm[distance], out_sems.at[distance]
        )
        copy.start()
        out_copies.append(copy)
    for copy in out_copies:
        copy.wait()


def contract_kernel(own_hbm, *refs):
    *in_refs, out_ref, own, sems = refs
    w_refs, p_refs = in_refs[: sems.shape[0]], in_refs[sems.shape[0] :]
    size = own.shape[0] // len(w_refs)
    copies = []
    for near in range(len(w_refs)):
        there = pl.ds(near * size, size)
        copies.append(pltpu.make_async_copy(own_hbm.at[there], own.at[there], sems.at[near]))
        copies[-1].start()
    galerkin = jnp.zeros((LANES, LANES), jnp.float32)
    for near, w_ref in enumerate(w_refs):
        copies[near].wait()
        for zh in range(size):
            piece = near * size + zh
            block = own[piece]
            for p_ref in p_refs:
                block += p_ref[piece].astype(jnp.float32)
            high = block.astype(jnp.bfloat16)
            low = (block - high.astype(jnp.float32)).astype(jnp.bfloat16)
            galerkin += jnp.dot(w_ref[zh], high, preferred_element_type=jnp.float32)
            galerkin += jnp.dot(w_ref[zh], low, preferred_element_type=jnp.float32)
    out_ref[:, 0, :] = galerkin[:HALF]
    out_ref[:, 1, :] = galerkin[HALF:TILE]
    corner = galerkin[TILE:]
    lane = lax.broadcasted_iota(jnp.int32, (HALF, LANES), 1)
    out_ref[:, 2, :] = jnp.where(lane < TILE, lane_swapped(corner[:HALF]), corner[HALF:])


def in_vmem(x):
    return pltpu.with_memory_space_constraint(x, pltpu.VMEM)


def exchanged(x, axes):
    return lax.all_to_all(x, axes, 0, 0, tiled=True)


def moved(x, axes, distance):
    peers = lax.axis_size(axes)
    return lax.ppermute(x, axes, [(i, (i + distance) % peers) for i in range(peers)])


def summed_over_all(x):
    peers, depth = lax.axis_size(ROW_Y), lax.axis_size(Z)
    piece = jnp.sum(exchanged(x, ROW_Y), axis=0)
    piece = jnp.sum(exchanged(jnp.broadcast_to(piece, (depth, *piece.shape)), Z), axis=0)
    return exchanged(jnp.broadcast_to(piece, (peers, *piece.shape)), ROW_Y)


def slot_table(a_rows, a_cols, a_count):
    rows, cols = a_rows.reshape(-1), a_cols.reshape(-1)
    f = rows % TILE
    zh, y, zl = f // 16, f // 4 % 4, f % 4
    y_distance = (y - lax.axis_index("y")) % 4
    z_distance = (lax.axis_index("zl") - zl) % 4
    place = ((y_distance * 4 + z_distance) * 4 + zh) * 2 + rows // TILE
    live = jnp.arange(rows.shape[0], dtype=jnp.int32) < a_count.reshape(())
    return jnp.where(live, place, 128) * 16 + cols


def coarse_blocks(a_tiles, a_rows, a_cols, a_count, p_tiles, p_cols):
    local_rows, _, slots, area = p_tiles.shape
    total_slots = a_tiles.shape[2]
    n_row, n_y = lax.axis_size("row"), lax.axis_size("y")
    n_zh, n_zl = lax.axis_size("zh"), lax.axis_size("zl")
    places = n_zh * n_zl * local_rows
    own_rows, own_turned = pl.pallas_call(
        window_kernel,
        out_shape=(
            jax.ShapeDtypeStruct((n_row, local_rows, TILE, LANES), jnp.bfloat16),
            jax.ShapeDtypeStruct((n_zh, LANES, LANES), jnp.bfloat16),
        ),
        grid_spec=pltpu.PrefetchScalarGridSpec(
            num_scalar_prefetch=1,
            in_specs=[VMEM],
            out_specs=[VMEM, VMEM],
            scratch_shapes=[
                pltpu.VMEM((local_rows, HALF, 8, LANES), jnp.float32),
                pltpu.VMEM((local_rows, TILE, LANES), jnp.float32),
            ],
        ),
        name="window",
    )(p_cols.reshape(local_rows, slots), p_tiles.reshape(local_rows, slots, area))
    column_window = exchanged(own_rows, "row").reshape(n_row * local_rows, TILE, LANES)
    unfolded = pl.pallas_call(
        unfold_kernel,
        out_shape=jax.ShapeDtypeStruct((total_slots, TILE, LANES), jnp.bfloat16),
        in_specs=[VMEM],
        out_specs=VMEM,
        scratch_shapes=[pltpu.VMEM((HALF, CHUNK, LANES), jnp.float32)],
        compiler_params=pltpu.CompilerParams(vmem_limit_bytes=8 << 20),
        name="unfold",
    )(in_vmem(a_tiles.reshape(total_slots, area)))
    pieces = [exchanged(own_turned, "zh")]
    products = pl.pallas_call(
        product_kernel,
        out_shape=[
            jax.ShapeDtypeStruct(
                (places, TILE, LANES), jnp.bfloat16 if distance else jnp.float32
            )
            for distance in range(n_y)
        ],
        grid_spec=pltpu.PrefetchScalarGridSpec(
            num_scalar_prefetch=1,
            in_specs=[VMEM, VMEM],
            out_specs=[ANY] * n_y,
            scratch_shapes=[
                pltpu.VMEM((n_y * places + 1, TILE, LANES), jnp.float32),
                pltpu.VMEM((n_y - 1, places, TILE, LANES), jnp.bfloat16),
                pltpu.SemaphoreType.DMA((n_y,)),
            ],
        ),
        name="product",
    )(slot_table(a_rows, a_cols, a_count), in_vmem(unfolded), in_vmem(column_window))
    own, gathered = products[0].reshape(-1, LANES, LANES), []
    for distance in range(1, n_y):
        gathered.append(moved(products[distance].reshape(-1, LANES, LANES), "y", distance))
    for distance in NEAR[1:]:
        pieces.append(moved(pieces[0], Z, distance))
    galerkin = pl.pallas_call(
        contract_kernel,
        out_shape=jax.ShapeDtypeStruct((HALF, 3, LANES), jnp.float32),
        in_specs=[ANY] + [VMEM] * (n_y - 1 + n_zl),
        out_specs=VMEM,
        scratch_shapes=[
            pltpu.VMEM((n_zh * n_zl, LANES, LANES), jnp.float32),
            pltpu.SemaphoreType.DMA((n_zl,)),
        ],
        compiler_params=pltpu.CompilerParams(vmem_limit_bytes=8 << 20),
        name="contract",
    )(
        pltpu.with_memory_space_constraint(own, pltpu.HBM),
        *[in_vmem(x) for x in (*pieces, *gathered)],
    )
    total = summed_over_all(galerkin)
    corner = jnp.concatenate([total[:, 2, :TILE], total[:, 2, TILE:]], axis=0)
    upper = jnp.concatenate([total[:, 0], total[:, 1]], axis=0)
    return jnp.concatenate([upper, corner], axis=1)


def solution(mesh):
    torus = Mesh(
        mesh.devices.reshape(mesh.shape["row"], 4, 4, mesh.shape["layer"]),
        ("row", "zh", "y", "zl"),
    )
    in_specs = (
        P("row", COL_LAYER, None, None),
        P("row", COL_LAYER, None),
        P("row", COL_LAYER, None),
        P("row", COL_LAYER),
        P("row", COL_LAYER, None, None),
        P("row", COL_LAYER, None),
    )
    return jax.shard_map(coarse_blocks, mesh=torus, in_specs=in_specs, out_specs=P(), check_vma=False)
```

```python
import jax
import jax.numpy as jnp
from jax import lax
from jax.experimental import pallas as pl
from jax.experimental.pallas import tpu as pltpu
from jax.sharding import Mesh
from jax.sharding import PartitionSpec as P

TILE = 64
HALF = TILE // 2
LANES = 2 * TILE
CHUNK = 16
GROUP = 4
NEAR = (0, 1, 2, 15)
COL_LAYER = ("zh", "y", "zl")
Z = ("zh", "zl")
ROW_Y = ("row", "y")
VMEM = pl.BlockSpec(memory_space=pltpu.VMEM)
ANY = pl.BlockSpec(memory_space=pl.ANY)


def lane_swapped(x):
    return pltpu.roll(x, TILE, axis=1)


def window_kernel(cols, p_ref, rows_ref, turned_ref, split, natural):
    local_rows, slots = cols.shape
    lane = lax.broadcasted_iota(jnp.int32, (HALF, LANES), 1)
    panel = lax.broadcasted_iota(jnp.int32, (8, slots), 0)
    slot = lax.broadcasted_iota(jnp.int32, (8, slots), 1)
    stacked = []
    for t in range(local_rows):
        chosen = jnp.zeros((8, slots), jnp.float32)
        for s in range(slots):
            chosen = jnp.where((slot == s) & (panel == cols[t, s]), 1.0, chosen)
        sums = jnp.dot(chosen.astype(jnp.bfloat16), p_ref[t], preferred_element_type=jnp.float32)
        for k in range(HALF):
            split[t, k] = sums[:, k * LANES : (k + 1) * LANES]
        first, second = split[t, :, 0, :], split[t, :, 1, :]
        even = jnp.where(lane < TILE, first, lane_swapped(second))
        odd = jnp.where(lane < TILE, lane_swapped(first), second)
        natural[t, pl.ds(0, HALF, stride=2)] = even
        natural[t, pl.ds(1, HALF, stride=2)] = odd
        stacked += [even, odd]
    rows = natural[...].astype(jnp.bfloat16)
    for r in range(rows_ref.shape[0]):
        rows_ref[r] = rows
    turned = jnp.concatenate(stacked, axis=0).T.astype(jnp.bfloat16)
    for z in range(turned_ref.shape[0]):
        turned_ref[z] = turned


def unfold_kernel(tiles, out_ref, split):
    def chunk(turn, carry):
        first = pl.multiple_of(turn * CHUNK, CHUNK)
        some = tiles[pl.ds(first, CHUNK), :].astype(jnp.float32)
        for k in range(HALF):
            split[k] = some[:, k * LANES : (k + 1) * LANES]
        for i in range(CHUNK):
            x = split[:, i, :]
            out_ref[first + i] = jnp.concatenate([x, lane_swapped(x)], axis=0).astype(jnp.bfloat16)
        return carry

    lax.fori_loop(0, tiles.shape[0] // CHUNK, chunk, 0)


def product_kernel(slots, tiles, window, *refs):
    own_ref, *out_hbm, total, rounded, out_sems = refs
    total[...] = jnp.zeros_like(total)

    def chunk(turn, carry):
        first = turn * CHUNK
        for g in range(0, CHUNK, GROUP):
            held = [slots[first + i] for i in range(g, g + GROUP)]
            parts = [
                jnp.dot(
                    tiles[first + g + i, :, :TILE],
                    window[held[i] & 15],
                    preferred_element_type=jnp.float32,
                )
                for i in range(GROUP)
            ]
            for i in range(GROUP):
                total[held[i] >> 4] += parts[i]
        return carry

    lax.fori_loop(0, tiles.shape[0] // CHUNK, chunk, 0)
    size = own_ref.shape[0]
    copies = []
    for distance, out in enumerate(out_hbm, 1):

        def store(turn, carry, distance=distance):
            rounded[distance - 1, turn] = total[distance * size + turn].astype(jnp.bfloat16)
            return carry

        lax.fori_loop(0, size, store, 0, unroll=8)
        copies.append(pltpu.make_async_copy(rounded.at[distance - 1], out, out_sems.at[distance - 1]))
        copies[-1].start()

    def keep(turn, carry):
        own_ref[turn] = total[turn]
        return carry

    lax.fori_loop(0, size, keep, 0, unroll=8)
    for copy in copies:
        copy.wait()


def contract_kernel(*refs):
    w_refs, (*p_refs, out_ref) = refs[: len(NEAR)], refs[len(NEAR) :]
    galerkin = jnp.zeros((LANES, LANES), jnp.float32)
    for near, w_ref in enumerate(w_refs):
        for zh in range(w_ref.shape[0]):
            piece = near * w_ref.shape[0] + zh
            block = sum(p_ref[piece].astype(jnp.float32) for p_ref in p_refs)
            high = block.astype(jnp.bfloat16)
            low = (block - high.astype(jnp.float32)).astype(jnp.bfloat16)
            galerkin += jnp.dot(w_ref[zh], high, preferred_element_type=jnp.float32)
            galerkin += jnp.dot(w_ref[zh], low, preferred_element_type=jnp.float32)
    out_ref[:, 0, :] = galerkin[:HALF]
    out_ref[:, 1, :] = galerkin[HALF:TILE]
    corner = galerkin[TILE:]
    lane = lax.broadcasted_iota(jnp.int32, (HALF, LANES), 1)
    out_ref[:, 2, :] = jnp.where(lane < TILE, lane_swapped(corner[:HALF]), corner[HALF:])


def in_vmem(x):
    return pltpu.with_memory_space_constraint(x, pltpu.VMEM)


def exchanged(x, axes):
    return lax.all_to_all(x, axes, 0, 0, tiled=True)


def moved(x, axes, distance):
    peers = lax.axis_size(axes)
    return lax.ppermute(x, axes, [(i, (i + distance) % peers) for i in range(peers)])


def summed_over_all(x):
    peers, depth = lax.axis_size(ROW_Y), lax.axis_size(Z)
    piece = jnp.sum(exchanged(x, ROW_Y), axis=0)
    piece = jnp.sum(exchanged(jnp.broadcast_to(piece, (depth, *piece.shape)), Z), axis=0)
    return exchanged(jnp.broadcast_to(piece, (peers, *piece.shape)), ROW_Y)


def slot_table(a_rows, a_cols, a_count):
    rows, cols = a_rows.reshape(-1), a_cols.reshape(-1)
    f = rows % TILE
    zh, y, zl = f // 16, f // 4 % 4, f % 4
    y_distance = (y - lax.axis_index("y")) % 4
    z_distance = (lax.axis_index("zl") - zl) % 4
    place = ((y_distance * 4 + z_distance) * 4 + zh) * 2 + rows // TILE
    live = jnp.arange(rows.shape[0], dtype=jnp.int32) < a_count.reshape(())
    return jnp.where(live, place, 128) * 16 + cols


def coarse_blocks(a_tiles, a_rows, a_cols, a_count, p_tiles, p_cols):
    local_rows, _, slots, area = p_tiles.shape
    total_slots = a_tiles.shape[2]
    n_row, n_y = lax.axis_size("row"), lax.axis_size("y")
    n_zh, n_zl = lax.axis_size("zh"), lax.axis_size("zl")
    places = n_zh * n_zl * local_rows
    own_rows, own_turned = pl.pallas_call(
        window_kernel,
        out_shape=(
            jax.ShapeDtypeStruct((n_row, local_rows, TILE, LANES), jnp.bfloat16),
            jax.ShapeDtypeStruct((n_zh, LANES, LANES), jnp.bfloat16),
        ),
        grid_spec=pltpu.PrefetchScalarGridSpec(
            num_scalar_prefetch=1,
            in_specs=[VMEM],
            out_specs=[VMEM, VMEM],
            scratch_shapes=[
                pltpu.VMEM((local_rows, HALF, 8, LANES), jnp.float32),
                pltpu.VMEM((local_rows, TILE, LANES), jnp.float32),
            ],
        ),
        name="window",
    )(p_cols.reshape(local_rows, slots), p_tiles.reshape(local_rows, slots, area))
    column_window = exchanged(own_rows, "row").reshape(n_row * local_rows, TILE, LANES)
    unfolded = pl.pallas_call(
        unfold_kernel,
        out_shape=jax.ShapeDtypeStruct((total_slots, TILE, LANES), jnp.bfloat16),
        in_specs=[VMEM],
        out_specs=VMEM,
        scratch_shapes=[pltpu.VMEM((HALF, CHUNK, LANES), jnp.float32)],
        compiler_params=pltpu.CompilerParams(vmem_limit_bytes=8 << 20),
        name="unfold",
    )(in_vmem(a_tiles.reshape(total_slots, area)))
    pieces = [exchanged(own_turned, "zh")]
    products = pl.pallas_call(
        product_kernel,
        out_shape=[jax.ShapeDtypeStruct((places, TILE, LANES), jnp.float32)]
        + [pltpu.HBM((places, TILE, LANES), jnp.bfloat16)] * (n_y - 1),
        grid_spec=pltpu.PrefetchScalarGridSpec(
            num_scalar_prefetch=1,
            in_specs=[VMEM, VMEM],
            out_specs=[VMEM] + [ANY] * (n_y - 1),
            scratch_shapes=[
                pltpu.VMEM((n_y * places + 1, TILE, LANES), jnp.float32),
                pltpu.VMEM((n_y - 1, places, TILE, LANES), jnp.bfloat16),
                pltpu.SemaphoreType.DMA((n_y - 1,)),
            ],
        ),
        compiler_params=pltpu.CompilerParams(vmem_limit_bytes=16 << 20),
        name="product",
    )(slot_table(a_rows, a_cols, a_count), in_vmem(unfolded), in_vmem(column_window))
    own, gathered = products[0].reshape(-1, LANES, LANES), []
    for distance in range(1, n_y):
        gathered.append(moved(products[distance].reshape(-1, LANES, LANES), "y", distance))
    for distance in NEAR[1:]:
        pieces.append(moved(pieces[0], Z, distance))
    galerkin = pl.pallas_call(
        contract_kernel,
        out_shape=jax.ShapeDtypeStruct((HALF, 3, LANES), jnp.float32),
        in_specs=[VMEM] * (n_y + n_zl),
        out_specs=VMEM,
        compiler_params=pltpu.CompilerParams(vmem_limit_bytes=8 << 20),
        name="contract",
    )(
        *[in_vmem(x) for x in (*pieces, own, *gathered)],
    )
    total = summed_over_all(galerkin)
    corner = jnp.concatenate([total[:, 2, :TILE], total[:, 2, TILE:]], axis=0)
    upper = jnp.concatenate([total[:, 0], total[:, 1]], axis=0)
    return jnp.concatenate([upper, corner], axis=1)


def solution(mesh):
    torus = Mesh(
        mesh.devices.reshape(mesh.shape["row"], 4, 4, mesh.shape["layer"]),
        ("row", "zh", "y", "zl"),
    )
    in_specs = (
        P("row", COL_LAYER, None, None),
        P("row", COL_LAYER, None),
        P("row", COL_LAYER, None),
        P("row", COL_LAYER),
        P("row", COL_LAYER, None, None),
        P("row", COL_LAYER, None),
    )
    return jax.shard_map(coarse_blocks, mesh=torus, in_specs=in_specs, out_specs=P(), check_vma=False)
```

```python
import jax
import jax.numpy as jnp
from jax import lax
from jax.experimental import pallas as pl
from jax.experimental.pallas import tpu as pltpu
from jax.sharding import Mesh
from jax.sharding import PartitionSpec as P

TILE = 64
HALF = TILE // 2
LANES = 2 * TILE
CHUNK = 16
GROUP = 4
NEAR = (0, 1, 2, 15)
COL_LAYER = ("zh", "y", "zl")
Z = ("zh", "zl")
ROW_Y = ("row", "y")
VMEM = pl.BlockSpec(memory_space=pltpu.VMEM)
ANY = pl.BlockSpec(memory_space=pl.ANY)


def lane_swapped(x):
    return pltpu.roll(x, TILE, axis=1)


def window_kernel(cols_ref, p_ref, rows_ref, turned_ref, split, natural):
    local_rows, slots = cols_ref.shape
    lane = lax.broadcasted_iota(jnp.int32, (HALF, LANES), 1)
    panel = lax.broadcasted_iota(jnp.int32, (8, slots), 0)
    stacked = []
    for t in range(local_rows):
        chosen = jnp.where(cols_ref[t : t + 1, :] == panel, 1.0, 0.0).astype(jnp.bfloat16)
        sums = jnp.dot(chosen, p_ref[t], preferred_element_type=jnp.float32)
        for k in range(HALF):
            split[t, k] = sums[:, k * LANES : (k + 1) * LANES]
        first, second = split[t, :, 0, :], split[t, :, 1, :]
        even = jnp.where(lane < TILE, first, lane_swapped(second))
        odd = jnp.where(lane < TILE, lane_swapped(first), second)
        natural[t, pl.ds(0, HALF, stride=2)] = even
        natural[t, pl.ds(1, HALF, stride=2)] = odd
        stacked += [even, odd]
    rows = natural[...].astype(jnp.bfloat16)
    for r in range(rows_ref.shape[0]):
        rows_ref[r] = rows
    turned = jnp.concatenate(stacked, axis=0).T.astype(jnp.bfloat16)
    for z in range(turned_ref.shape[0]):
        turned_ref[z] = turned


def unfold_kernel(tiles, out_ref, split):
    def chunk(turn, carry):
        first = pl.multiple_of(turn * CHUNK, CHUNK)
        some = tiles[pl.ds(first, CHUNK), :].astype(jnp.float32)
        for k in range(HALF):
            split[k] = some[:, k * LANES : (k + 1) * LANES]
        for i in range(CHUNK):
            x = split[:, i, :]
            out_ref[first + i] = jnp.concatenate([x, lane_swapped(x)], axis=0).astype(jnp.bfloat16)
        return carry

    lax.fori_loop(0, tiles.shape[0] // CHUNK, chunk, 0)


def product_kernel(slots_hbm, tiles, window, *refs):
    own_ref, *out_hbm, slots, total, rounded, slots_sem, out_sems = refs
    slots_copy = pltpu.make_async_copy(slots_hbm, slots, slots_sem)
    slots_copy.start()
    total[...] = jnp.zeros_like(total)
    slots_copy.wait()

    def chunk(turn, carry):
        first = turn * CHUNK
        for g in range(0, CHUNK, GROUP):
            held = [slots[first + i] for i in range(g, g + GROUP)]
            parts = [
                jnp.dot(
                    tiles[first + g + i, :, :TILE],
                    window[held[i] & 15],
                    preferred_element_type=jnp.float32,
                )
                for i in range(GROUP)
            ]
            for i in range(GROUP):
                total[held[i] >> 4] += parts[i]
        return carry

    lax.fori_loop(0, tiles.shape[0] // CHUNK, chunk, 0)
    size = own_ref.shape[0]
    copies = []
    for distance, out in enumerate(out_hbm, 1):

        def store(turn, carry, distance=distance):
            rounded[distance - 1, turn] = total[distance * size + turn].astype(jnp.bfloat16)
            return carry

        lax.fori_loop(0, size, store, 0, unroll=8)
        copies.append(pltpu.make_async_copy(rounded.at[distance - 1], out, out_sems.at[distance - 1]))
        copies[-1].start()

    def keep(turn, carry):
        own_ref[turn] = total[turn]
        return carry

    lax.fori_loop(0, size, keep, 0, unroll=8)
    for copy in copies:
        copy.wait()


def contract_kernel(*refs):
    w_refs, (*p_refs, out_ref) = refs[: len(NEAR)], refs[len(NEAR) :]
    galerkin = jnp.zeros((LANES, LANES), jnp.float32)
    for near, w_ref in enumerate(w_refs):
        for zh in range(w_ref.shape[0]):
            piece = near * w_ref.shape[0] + zh
            block = sum(p_ref[piece].astype(jnp.float32) for p_ref in p_refs)
            high = block.astype(jnp.bfloat16)
            low = (block - high.astype(jnp.float32)).astype(jnp.bfloat16)
            galerkin += jnp.dot(w_ref[zh], high, preferred_element_type=jnp.float32)
            galerkin += jnp.dot(w_ref[zh], low, preferred_element_type=jnp.float32)
    out_ref[:, 0, :] = galerkin[:HALF]
    out_ref[:, 1, :] = galerkin[HALF:TILE]
    corner = galerkin[TILE:]
    lane = lax.broadcasted_iota(jnp.int32, (HALF, LANES), 1)
    out_ref[:, 2, :] = jnp.where(lane < TILE, lane_swapped(corner[:HALF]), corner[HALF:])


def in_vmem(x):
    return pltpu.with_memory_space_constraint(x, pltpu.VMEM)


def exchanged(x, axes):
    return lax.all_to_all(x, axes, 0, 0, tiled=True)


def moved(x, axes, distance):
    peers = lax.axis_size(axes)
    return lax.ppermute(x, axes, [(i, (i + distance) % peers) for i in range(peers)])


def summed_over_all(x):
    peers, depth = lax.axis_size(ROW_Y), lax.axis_size(Z)
    piece = jnp.sum(exchanged(x, ROW_Y), axis=0)
    piece = jnp.sum(exchanged(jnp.broadcast_to(piece, (depth, *piece.shape)), Z), axis=0)
    return exchanged(jnp.broadcast_to(piece, (peers, *piece.shape)), ROW_Y)


def slot_table(a_rows, a_cols, a_count):
    rows, cols = a_rows.reshape(-1), a_cols.reshape(-1)
    f = rows % TILE
    zh, y, zl = f // 16, f // 4 % 4, f % 4
    y_distance = (y - lax.axis_index("y")) % 4
    z_distance = (lax.axis_index("zl") - zl) % 4
    place = ((y_distance * 4 + z_distance) * 4 + zh) * 2 + rows // TILE
    live = jnp.arange(rows.shape[0], dtype=jnp.int32) < a_count.reshape(())
    return jnp.where(live, place, 128) * 16 + cols


def coarse_blocks(a_tiles, a_rows, a_cols, a_count, p_tiles, p_cols):
    local_rows, _, slots, area = p_tiles.shape
    total_slots = a_tiles.shape[2]
    n_row, n_y = lax.axis_size("row"), lax.axis_size("y")
    n_zh, n_zl = lax.axis_size("zh"), lax.axis_size("zl")
    places = n_zh * n_zl * local_rows
    own_rows, own_turned = pl.pallas_call(
        window_kernel,
        out_shape=(
            jax.ShapeDtypeStruct((n_row, local_rows, TILE, LANES), jnp.bfloat16),
            jax.ShapeDtypeStruct((n_zh, LANES, LANES), jnp.bfloat16),
        ),
        in_specs=[VMEM, VMEM],
        out_specs=[VMEM, VMEM],
        scratch_shapes=[
            pltpu.VMEM((local_rows, HALF, 8, LANES), jnp.float32),
            pltpu.VMEM((local_rows, TILE, LANES), jnp.float32),
        ],
        name="window",
    )(p_cols.reshape(local_rows, slots), p_tiles.reshape(local_rows, slots, area))
    column_window = exchanged(own_rows, "row").reshape(n_row * local_rows, TILE, LANES)
    unfolded = pl.pallas_call(
        unfold_kernel,
        out_shape=jax.ShapeDtypeStruct((total_slots, TILE, LANES), jnp.bfloat16),
        in_specs=[VMEM],
        out_specs=VMEM,
        scratch_shapes=[pltpu.VMEM((HALF, CHUNK, LANES), jnp.float32)],
        compiler_params=pltpu.CompilerParams(vmem_limit_bytes=8 << 20),
        name="unfold",
    )(in_vmem(a_tiles.reshape(total_slots, area)))
    pieces = [exchanged(own_turned, "zh")]
    products = pl.pallas_call(
        product_kernel,
        out_shape=[jax.ShapeDtypeStruct((places, TILE, LANES), jnp.float32)]
        + [pltpu.HBM((places, TILE, LANES), jnp.bfloat16)] * (n_y - 1),
        in_specs=[ANY, VMEM, VMEM],
        out_specs=[VMEM] + [ANY] * (n_y - 1),
        scratch_shapes=[
            pltpu.SMEM((total_slots,), jnp.int32),
            pltpu.VMEM((n_y * places + 1, TILE, LANES), jnp.float32),
            pltpu.VMEM((n_y - 1, places, TILE, LANES), jnp.bfloat16),
            pltpu.SemaphoreType.DMA,
            pltpu.SemaphoreType.DMA((n_y - 1,)),
        ],
        compiler_params=pltpu.CompilerParams(vmem_limit_bytes=16 << 20),
        name="product",
    )(slot_table(a_rows, a_cols, a_count), in_vmem(unfolded), in_vmem(column_window))
    own, gathered = products[0].reshape(-1, LANES, LANES), []
    for distance in range(1, n_y):
        gathered.append(moved(products[distance].reshape(-1, LANES, LANES), "y", distance))
    for distance in NEAR[1:]:
        pieces.append(moved(pieces[0], Z, distance))
    galerkin = pl.pallas_call(
        contract_kernel,
        out_shape=jax.ShapeDtypeStruct((HALF, 3, LANES), jnp.float32),
        in_specs=[VMEM] * (n_y + n_zl),
        out_specs=VMEM,
        compiler_params=pltpu.CompilerParams(vmem_limit_bytes=8 << 20),
        name="contract",
    )(
        *[in_vmem(x) for x in (*pieces, own, *gathered)],
    )
    total = summed_over_all(galerkin)
    corner = jnp.concatenate([total[:, 2, :TILE], total[:, 2, TILE:]], axis=0)
    upper = jnp.concatenate([total[:, 0], total[:, 1]], axis=0)
    return jnp.concatenate([upper, corner], axis=1)


def solution(mesh):
    torus = Mesh(
        mesh.devices.reshape(mesh.shape["row"], 4, 4, mesh.shape["layer"]),
        ("row", "zh", "y", "zl"),
    )
    in_specs = (
        P("row", COL_LAYER, None, None),
        P("row", COL_LAYER, None),
        P("row", COL_LAYER, None),
        P("row", COL_LAYER),
        P("row", COL_LAYER, None, None),
        P("row", COL_LAYER, None),
    )
    return jax.shard_map(coarse_blocks, mesh=torus, in_specs=in_specs, out_specs=P(), check_vma=False)
```

```python
import jax
import jax.numpy as jnp
from jax import lax
from jax.experimental import pallas as pl
from jax.experimental.pallas import tpu as pltpu
from jax.sharding import Mesh
from jax.sharding import PartitionSpec as P

TILE = 64
HALF = TILE // 2
LANES = 2 * TILE
CHUNK = 16
GROUP = 4
NEAR = (0, 1)
COL_LAYER = ("zh", "y", "zm", "z0")
Z = ("zh", "zm", "z0")
FAR = ("zh", "zm")
ROW_Y = ("row", "y")
VMEM = pl.BlockSpec(memory_space=pltpu.VMEM)
ANY = pl.BlockSpec(memory_space=pl.ANY)


def lane_swapped(x):
    return pltpu.roll(x, TILE, axis=1)


def window_kernel(cols_ref, p_ref, rows_ref, turned_ref, split, natural):
    local_rows, slots = cols_ref.shape
    lane = lax.broadcasted_iota(jnp.int32, (HALF, LANES), 1)
    panel = lax.broadcasted_iota(jnp.int32, (8, slots), 0)
    stacked = []
    for t in range(local_rows):
        chosen = jnp.where(cols_ref[t : t + 1, :] == panel, 1.0, 0.0).astype(jnp.bfloat16)
        sums = jnp.dot(chosen, p_ref[t], preferred_element_type=jnp.float32)
        for k in range(HALF):
            split[t, k] = sums[:, k * LANES : (k + 1) * LANES]
        first, second = split[t, :, 0, :], split[t, :, 1, :]
        even = jnp.where(lane < TILE, first, lane_swapped(second))
        odd = jnp.where(lane < TILE, lane_swapped(first), second)
        natural[t, pl.ds(0, HALF, stride=2)] = even
        natural[t, pl.ds(1, HALF, stride=2)] = odd
        stacked += [even, odd]
    rows = natural[...].astype(jnp.bfloat16)
    for r in range(rows_ref.shape[0]):
        rows_ref[r] = rows
    turned = jnp.concatenate(stacked, axis=0).T.astype(jnp.bfloat16)
    for z in range(turned_ref.shape[0]):
        turned_ref[z] = turned


def unfold_kernel(tiles, out_ref, split):
    def chunk(turn, carry):
        first = pl.multiple_of(turn * CHUNK, CHUNK)
        some = tiles[pl.ds(first, CHUNK), :].astype(jnp.float32)
        for k in range(HALF):
            split[k] = some[:, k * LANES : (k + 1) * LANES]
        for i in range(CHUNK):
            x = split[:, i, :]
            out_ref[first + i] = jnp.concatenate([x, lane_swapped(x)], axis=0).astype(jnp.bfloat16)
        return carry

    lax.fori_loop(0, tiles.shape[0] // CHUNK, chunk, 0)


def product_kernel(slots_hbm, tiles, window, *refs):
    own_ref, *out_hbm, slots, total, rounded, slots_sem, out_sems = refs
    slots_copy = pltpu.make_async_copy(slots_hbm, slots, slots_sem)
    slots_copy.start()
    total[...] = jnp.zeros_like(total)
    slots_copy.wait()

    def chunk(turn, carry):
        first = turn * CHUNK
        for g in range(0, CHUNK, GROUP):
            held = [slots[first + i] for i in range(g, g + GROUP)]
            parts = [
                jnp.dot(
                    tiles[first + g + i, :, :TILE],
                    window[held[i] & 15],
                    preferred_element_type=jnp.float32,
                )
                for i in range(GROUP)
            ]
            for i in range(GROUP):
                total[held[i] >> 4] += parts[i]
        return carry

    lax.fori_loop(0, tiles.shape[0] // CHUNK, chunk, 0)
    size = own_ref.shape[0]
    copies = []
    for distance, out in enumerate(out_hbm, 1):

        def store(turn, carry, distance=distance):
            rounded[distance - 1, turn] = total[distance * size + turn].astype(jnp.bfloat16)
            return carry

        lax.fori_loop(0, size, store, 0, unroll=8)
        copies.append(pltpu.make_async_copy(rounded.at[distance - 1], out, out_sems.at[distance - 1]))
        copies[-1].start()

    def keep(turn, carry):
        own_ref[turn] = total[turn]
        return carry

    lax.fori_loop(0, size, keep, 0, unroll=8)
    for copy in copies:
        copy.wait()


def contract_kernel(*refs):
    w_refs, (*p_refs, out_ref) = refs[: len(NEAR)], refs[len(NEAR) :]
    galerkin = jnp.zeros((LANES, LANES), jnp.float32)
    for near, w_ref in enumerate(w_refs):
        for zh in range(w_ref.shape[0]):
            piece = near * w_ref.shape[0] + zh
            block = sum(p_ref[piece].astype(jnp.float32) for p_ref in p_refs)
            high = block.astype(jnp.bfloat16)
            low = (block - high.astype(jnp.float32)).astype(jnp.bfloat16)
            galerkin += jnp.dot(w_ref[zh], high, preferred_element_type=jnp.float32)
            galerkin += jnp.dot(w_ref[zh], low, preferred_element_type=jnp.float32)
    out_ref[:, 0, :] = galerkin[:HALF]
    out_ref[:, 1, :] = galerkin[HALF:TILE]
    corner = galerkin[TILE:]
    lane = lax.broadcasted_iota(jnp.int32, (HALF, LANES), 1)
    out_ref[:, 2, :] = jnp.where(lane < TILE, lane_swapped(corner[:HALF]), corner[HALF:])


def in_vmem(x):
    return pltpu.with_memory_space_constraint(x, pltpu.VMEM)


def exchanged(x, axes):
    return lax.all_to_all(x, axes, 0, 0, tiled=True)


def moved(x, axes, distance):
    rows, peers = lax.axis_size("row"), lax.axis_size(axes)
    pairs = [
        (row * peers + i, row * peers + (i + distance * (1 - 2 * (row % 2))) % peers)
        for row in range(rows)
        for i in range(peers)
    ]
    return lax.ppermute(x, ("row", *axes), pairs)


def summed_over_all(x):
    peers, depth = lax.axis_size(ROW_Y), lax.axis_size(Z)
    piece = jnp.sum(exchanged(x, ROW_Y), axis=0)
    piece = jnp.sum(exchanged(jnp.broadcast_to(piece, (depth, *piece.shape)), Z), axis=0)
    return exchanged(jnp.broadcast_to(piece, (peers, *piece.shape)), ROW_Y)


def slot_table(a_rows, a_cols, a_count):
    rows, cols = a_rows.reshape(-1), a_cols.reshape(-1)
    f = rows % TILE
    zh, y, zm, z0 = f // 16, f // 4 % 4, f // 2 % 2, f % 2
    way = 1 - 2 * (lax.axis_index("row") % 2)
    y_distance = (way * (y - lax.axis_index("y"))) % 4
    other = (z0 + lax.axis_index("z0")) % 2
    place = ((y_distance * 2 + other) * 8 + zh * 2 + zm) * 2 + rows // TILE
    live = jnp.arange(rows.shape[0], dtype=jnp.int32) < a_count.reshape(())
    return jnp.where(live, place, 128) * 16 + cols


def coarse_blocks(a_tiles, a_rows, a_cols, a_count, p_tiles, p_cols):
    local_rows, _, slots, area = p_tiles.shape
    total_slots = a_tiles.shape[2]
    n_row, n_y = lax.axis_size("row"), lax.axis_size("y")
    n_far = lax.axis_size(FAR)
    places = lax.axis_size(Z) * local_rows
    own_rows, own_turned = pl.pallas_call(
        window_kernel,
        out_shape=(
            jax.ShapeDtypeStruct((n_row, local_rows, TILE, LANES), jnp.bfloat16),
            jax.ShapeDtypeStruct((n_far, LANES, LANES), jnp.bfloat16),
        ),
        in_specs=[VMEM, VMEM],
        out_specs=[VMEM, VMEM],
        scratch_shapes=[
            pltpu.VMEM((local_rows, HALF, 8, LANES), jnp.float32),
            pltpu.VMEM((local_rows, TILE, LANES), jnp.float32),
        ],
        name="window",
    )(p_cols.reshape(local_rows, slots), p_tiles.reshape(local_rows, slots, area))
    column_window = exchanged(own_rows, "row").reshape(n_row * local_rows, TILE, LANES)
    unfolded = pl.pallas_call(
        unfold_kernel,
        out_shape=jax.ShapeDtypeStruct((total_slots, TILE, LANES), jnp.bfloat16),
        in_specs=[VMEM],
        out_specs=VMEM,
        scratch_shapes=[pltpu.VMEM((HALF, CHUNK, LANES), jnp.float32)],
        compiler_params=pltpu.CompilerParams(vmem_limit_bytes=8 << 20),
        name="unfold",
    )(in_vmem(a_tiles.reshape(total_slots, area)))
    pieces = [exchanged(own_turned, FAR)]
    products = pl.pallas_call(
        product_kernel,
        out_shape=[jax.ShapeDtypeStruct((places, TILE, LANES), jnp.float32)]
        + [pltpu.HBM((places, TILE, LANES), jnp.bfloat16)] * (n_y - 1),
        in_specs=[ANY, VMEM, VMEM],
        out_specs=[VMEM] + [ANY] * (n_y - 1),
        scratch_shapes=[
            pltpu.SMEM((total_slots,), jnp.int32),
            pltpu.VMEM((n_y * places + 1, TILE, LANES), jnp.float32),
            pltpu.VMEM((n_y - 1, places, TILE, LANES), jnp.bfloat16),
            pltpu.SemaphoreType.DMA,
            pltpu.SemaphoreType.DMA((n_y - 1,)),
        ],
        compiler_params=pltpu.CompilerParams(vmem_limit_bytes=16 << 20),
        name="product",
    )(slot_table(a_rows, a_cols, a_count), in_vmem(unfolded), in_vmem(column_window))
    own, gathered = products[0].reshape(-1, LANES, LANES), []
    for distance in range(1, n_y):
        gathered.append(moved(products[distance].reshape(-1, LANES, LANES), ("y",), distance))
    for distance in NEAR[1:]:
        pieces.append(moved(pieces[0], Z, distance))
    galerkin = pl.pallas_call(
        contract_kernel,
        out_shape=jax.ShapeDtypeStruct((HALF, 3, LANES), jnp.float32),
        in_specs=[VMEM] * (n_y + len(NEAR)),
        out_specs=VMEM,
        compiler_params=pltpu.CompilerParams(vmem_limit_bytes=8 << 20),
        name="contract",
    )(
        *[in_vmem(x) for x in (*pieces, own, *gathered)],
    )
    total = summed_over_all(galerkin)
    corner = jnp.concatenate([total[:, 2, :TILE], total[:, 2, TILE:]], axis=0)
    upper = jnp.concatenate([total[:, 0], total[:, 1]], axis=0)
    return jnp.concatenate([upper, corner], axis=1)


def solution(mesh):
    torus = Mesh(
        mesh.devices.reshape(mesh.shape["row"], 4, 4, 2, 2),
        ("row", "zh", "y", "zm", "z0"),
    )
    in_specs = (
        P("row", COL_LAYER, None, None),
        P("row", COL_LAYER, None),
        P("row", COL_LAYER, None),
        P("row", COL_LAYER),
        P("row", COL_LAYER, None, None),
        P("row", COL_LAYER, None),
    )
    return jax.shard_map(coarse_blocks, mesh=torus, in_specs=in_specs, out_specs=P(), check_vma=False)
```

```python
import jax
import jax.numpy as jnp
from jax import lax
from jax.experimental import pallas as pl
from jax.experimental.pallas import tpu as pltpu
from jax.sharding import Mesh
from jax.sharding import PartitionSpec as P

TILE = 64
HALF = TILE // 2
LANES = 2 * TILE
CHUNK = 16
GROUP = 4
NEAR = (0, 1)
COL_LAYER = ("zh", "y", "zm", "z0")
Z = ("zh", "zm", "z0")
FAR = ("zm", "zh")
SUM_Z = ("z0", "zm", "zh")
ROW_Y = ("row", "y")
VMEM = pl.BlockSpec(memory_space=pltpu.VMEM)
ANY = pl.BlockSpec(memory_space=pl.ANY)


def lane_swapped(x):
    return pltpu.roll(x, TILE, axis=1)


def window_kernel(cols_ref, p_ref, rows_ref, turned_ref, split, natural):
    local_rows, slots = cols_ref.shape
    lane = lax.broadcasted_iota(jnp.int32, (HALF, LANES), 1)
    panel = lax.broadcasted_iota(jnp.int32, (8, slots), 0)
    stacked = []
    for t in range(local_rows):
        chosen = jnp.where(cols_ref[t : t + 1, :] == panel, 1.0, 0.0).astype(jnp.bfloat16)
        sums = jnp.dot(chosen, p_ref[t], preferred_element_type=jnp.float32)
        for k in range(HALF):
            split[t, k] = sums[:, k * LANES : (k + 1) * LANES]
        first, second = split[t, :, 0, :], split[t, :, 1, :]
        even = jnp.where(lane < TILE, first, lane_swapped(second))
        odd = jnp.where(lane < TILE, lane_swapped(first), second)
        natural[t, pl.ds(0, HALF, stride=2)] = even
        natural[t, pl.ds(1, HALF, stride=2)] = odd
        stacked += [even, odd]
    rows = natural[...].astype(jnp.bfloat16)
    for r in range(rows_ref.shape[0]):
        rows_ref[r] = rows
    turned = jnp.concatenate(stacked, axis=0).T.astype(jnp.bfloat16)
    for z in range(turned_ref.shape[0]):
        turned_ref[z] = turned


def unfold_kernel(tiles, out_ref, split):
    def chunk(turn, carry):
        first = pl.multiple_of(turn * CHUNK, CHUNK)
        some = tiles[pl.ds(first, CHUNK), :].astype(jnp.float32)
        for k in range(HALF):
            split[k] = some[:, k * LANES : (k + 1) * LANES]
        for i in range(CHUNK):
            x = split[:, i, :]
            out_ref[first + i] = jnp.concatenate([x, lane_swapped(x)], axis=0).astype(jnp.bfloat16)
        return carry

    lax.fori_loop(0, tiles.shape[0] // CHUNK, chunk, 0)


def product_kernel(slots_hbm, tiles, window, *refs):
    own_ref, *out_hbm, slots, total, rounded, slots_sem, out_sems = refs
    slots_copy = pltpu.make_async_copy(slots_hbm, slots, slots_sem)
    slots_copy.start()
    total[...] = jnp.zeros_like(total)
    slots_copy.wait()

    def chunk(turn, carry):
        first = turn * CHUNK
        for g in range(0, CHUNK, GROUP):
            held = [slots[first + i] for i in range(g, g + GROUP)]
            parts = [
                jnp.dot(
                    tiles[first + g + i, :, :TILE],
                    window[held[i] & 15],
                    preferred_element_type=jnp.float32,
                )
                for i in range(GROUP)
            ]
            for i in range(GROUP):
                total[held[i] >> 4] += parts[i]
        return carry

    lax.fori_loop(0, tiles.shape[0] // CHUNK, chunk, 0)
    size = own_ref.shape[0]
    copies = []
    for distance, out in enumerate(out_hbm, 1):

        def store(turn, carry, distance=distance):
            rounded[distance - 1, turn] = total[distance * size + turn].astype(jnp.bfloat16)
            return carry

        lax.fori_loop(0, size, store, 0, unroll=8)
        copies.append(pltpu.make_async_copy(rounded.at[distance - 1], out, out_sems.at[distance - 1]))
        copies[-1].start()

    def keep(turn, carry):
        own_ref[turn] = total[turn]
        return carry

    lax.fori_loop(0, size, keep, 0, unroll=8)
    for copy in copies:
        copy.wait()


def contract_kernel(*refs):
    w_refs, (*p_refs, out_ref) = refs[: len(NEAR)], refs[len(NEAR) :]
    galerkin = jnp.zeros((LANES, LANES), jnp.float32)
    for near, w_ref in enumerate(w_refs):
        for zh in range(w_ref.shape[0]):
            piece = near * w_ref.shape[0] + zh
            block = sum(p_ref[piece].astype(jnp.float32) for p_ref in p_refs)
            high = block.astype(jnp.bfloat16)
            low = (block - high.astype(jnp.float32)).astype(jnp.bfloat16)
            galerkin += jnp.dot(w_ref[zh], high, preferred_element_type=jnp.float32)
            galerkin += jnp.dot(w_ref[zh], low, preferred_element_type=jnp.float32)
    out_ref[:, 0, :] = galerkin[:HALF]
    out_ref[:, 1, :] = galerkin[HALF:TILE]
    corner = galerkin[TILE:]
    lane = lax.broadcasted_iota(jnp.int32, (HALF, LANES), 1)
    out_ref[:, 2, :] = jnp.where(lane < TILE, lane_swapped(corner[:HALF]), corner[HALF:])


def in_vmem(x):
    return pltpu.with_memory_space_constraint(x, pltpu.VMEM)


def exchanged(x, axes):
    return lax.all_to_all(x, axes, 0, 0, tiled=True)


def moved(x, axes, distance):
    rows, peers = lax.axis_size("row"), lax.axis_size(axes)
    pairs = [
        (row * peers + i, row * peers + (i + distance * (1 - 2 * (row % 2))) % peers)
        for row in range(rows)
        for i in range(peers)
    ]
    return lax.ppermute(x, ("row", *axes), pairs)


def summed_over_all(x):
    peers, depth = lax.axis_size(ROW_Y), lax.axis_size(Z)
    piece = jnp.sum(exchanged(x, ROW_Y), axis=0)
    piece = jnp.sum(exchanged(jnp.broadcast_to(piece, (depth, *piece.shape)), SUM_Z), axis=0)
    return exchanged(jnp.broadcast_to(piece, (peers, *piece.shape)), ROW_Y)


def slot_table(a_rows, a_cols, a_count):
    rows, cols = a_rows.reshape(-1), a_cols.reshape(-1)
    f = rows % TILE
    zh, y, zm, z0 = f // 16, f // 4 % 4, f // 2 % 2, f % 2
    way = 1 - 2 * (lax.axis_index("row") % 2)
    y_distance = (way * (y - lax.axis_index("y"))) % 4
    other = (z0 + lax.axis_index("z0")) % 2
    place = ((y_distance * 2 + other) * 8 + zm * 4 + zh) * 2 + rows // TILE
    live = jnp.arange(rows.shape[0], dtype=jnp.int32) < a_count.reshape(())
    return jnp.where(live, place, 128) * 16 + cols


def coarse_blocks(a_tiles, a_rows, a_cols, a_count, p_tiles, p_cols):
    local_rows, _, slots, area = p_tiles.shape
    total_slots = a_tiles.shape[2]
    n_row, n_y = lax.axis_size("row"), lax.axis_size("y")
    n_far = lax.axis_size(FAR)
    places = lax.axis_size(Z) * local_rows
    own_rows, own_turned = pl.pallas_call(
        window_kernel,
        out_shape=(
            jax.ShapeDtypeStruct((n_row, local_rows, TILE, LANES), jnp.bfloat16),
            jax.ShapeDtypeStruct((n_far, LANES, LANES), jnp.bfloat16),
        ),
        in_specs=[VMEM, VMEM],
        out_specs=[VMEM, VMEM],
        scratch_shapes=[
            pltpu.VMEM((local_rows, HALF, 8, LANES), jnp.float32),
            pltpu.VMEM((local_rows, TILE, LANES), jnp.float32),
        ],
        name="window",
    )(p_cols.reshape(local_rows, slots), p_tiles.reshape(local_rows, slots, area))
    column_window = exchanged(own_rows, "row").reshape(n_row * local_rows, TILE, LANES)
    unfolded = pl.pallas_call(
        unfold_kernel,
        out_shape=jax.ShapeDtypeStruct((total_slots, TILE, LANES), jnp.bfloat16),
        in_specs=[VMEM],
        out_specs=VMEM,
        scratch_shapes=[pltpu.VMEM((HALF, CHUNK, LANES), jnp.float32)],
        compiler_params=pltpu.CompilerParams(vmem_limit_bytes=8 << 20),
        name="unfold",
    )(in_vmem(a_tiles.reshape(total_slots, area)))
    pieces = [exchanged(own_turned, FAR)]
    products = pl.pallas_call(
        product_kernel,
        out_shape=[jax.ShapeDtypeStruct((places, TILE, LANES), jnp.float32)]
        + [pltpu.HBM((places, TILE, LANES), jnp.bfloat16)] * (n_y - 1),
        in_specs=[ANY, VMEM, VMEM],
        out_specs=[VMEM] + [ANY] * (n_y - 1),
        scratch_shapes=[
            pltpu.SMEM((total_slots,), jnp.int32),
            pltpu.VMEM((n_y * places + 1, TILE, LANES), jnp.float32),
            pltpu.VMEM((n_y - 1, places, TILE, LANES), jnp.bfloat16),
            pltpu.SemaphoreType.DMA,
            pltpu.SemaphoreType.DMA((n_y - 1,)),
        ],
        compiler_params=pltpu.CompilerParams(vmem_limit_bytes=16 << 20),
        name="product",
    )(slot_table(a_rows, a_cols, a_count), in_vmem(unfolded), in_vmem(column_window))
    own, gathered = products[0].reshape(-1, LANES, LANES), []
    for distance in range(1, n_y):
        gathered.append(moved(products[distance].reshape(-1, LANES, LANES), ("y",), distance))
    for distance in NEAR[1:]:
        pieces.append(moved(pieces[0], Z, distance))
    galerkin = pl.pallas_call(
        contract_kernel,
        out_shape=jax.ShapeDtypeStruct((HALF, 3, LANES), jnp.float32),
        in_specs=[VMEM] * (n_y + len(NEAR)),
        out_specs=VMEM,
        compiler_params=pltpu.CompilerParams(vmem_limit_bytes=8 << 20),
        name="contract",
    )(
        *[in_vmem(x) for x in (*pieces, own, *gathered)],
    )
    total = summed_over_all(galerkin)
    corner = jnp.concatenate([total[:, 2, :TILE], total[:, 2, TILE:]], axis=0)
    upper = jnp.concatenate([total[:, 0], total[:, 1]], axis=0)
    return jnp.concatenate([upper, corner], axis=1)


def solution(mesh):
    torus = Mesh(
        mesh.devices.reshape(mesh.shape["row"], 4, 4, 2, 2),
        ("row", "zh", "y", "zm", "z0"),
    )
    in_specs = (
        P("row", COL_LAYER, None, None),
        P("row", COL_LAYER, None),
        P("row", COL_LAYER, None),
        P("row", COL_LAYER),
        P("row", COL_LAYER, None, None),
        P("row", COL_LAYER, None),
    )
    return jax.shard_map(coarse_blocks, mesh=torus, in_specs=in_specs, out_specs=P(), check_vma=False)
```
